32 devices in a mesh: groups: 2 (over x), seq: 16 (over z, y, core).
Axes of the slice: x: 2, y: 2, z: 4, core: 2. Of those that a mesh axis runs over, the one named last changes fastest.
Arguments:
- queries: bfloat16 [4096, 2048], P(('groups', 'seq')), parts along dimension 0, may hold values from -140 to 140
- keys: bfloat16 [4096, 2048], P(('groups', 'seq')), parts along dimension 0, may hold values from -6.25 to 6.25
- values: bfloat16 [4096, 2048], P(('groups', 'seq')), parts along dimension 0, may hold values from -6 to 6
- grad_out: bfloat16 [4096, 2048], P(('groups', 'seq')), parts along dimension 0, may hold values from -6 to 6
- partners: int32 [32, 16, 3], P(('groups', 'seq')), parts along dimension 0, may hold values from 0 to 15, all different within a row; in each aligned block of 16 rows (0 to 15, 16 to 31, ..., all dimensions but the last counted through in order) at most 3 rows name the same one
Outputs:
- grad_queries: bfloat16 [4096, 2048], P(('groups', 'seq')), parts along dimension 0
- grad_keys: bfloat16 [4096, 2048], P(('groups', 'seq')), parts along dimension 0
- grad_values: bfloat16 [4096, 2048], P(('groups', 'seq')), parts along dimension 0
The draws below stay inside these ranges and needn't reach their ends.
There are 2 independent parts, one for each index of `groups`. The reference program is written for one: setup_inputs(seed, part) draws one part's arguments, and reference() takes and returns one part's arrays. A program takes and returns all parts, laid end to end along the dimension named above; each array names one. Nothing has to cross between parts.
Inputs may be any that keep to these rules, and one draw needn't show every extreme that they name: In the 16 head rows of one query block, no block is named more than 3 times, and some block is named exactly 3 times; the 3 partners of one head are different blocks.
All inputs are finite; a program needn't handle non-finite values.
Results may differ from the reference program's by a relative error of at most 0.01.
Values may be sent and summed in bfloat16 or wider, within the bound.
A program may use at most 128 MiB of HBM per device.

```python
import math
import jax
import jax.numpy as jnp
import numpy as np
from jax import lax

H = 16
HD = 128
BLK = 128
BLOCKS = 16
TOKENS = 2048
MOST = 3


def paired_fields(key):
    base_key = jax.random.fold_in(key, 11)
    width = H * HD
    key_field = jnp.clip(jax.random.normal(jax.random.fold_in(base_key, 1), (TOKENS, width), jnp.float32), -6.0, 6.0)
    query_field = jnp.clip(jax.random.normal(jax.random.fold_in(base_key, 2), (TOKENS, width), jnp.float32), -6.0, 6.0)
    return (query_field, key_field)


def draw_queries(key, part):
    return paired_fields(key)[0].astype(jnp.bfloat16)


def draw_keys(key, part):
    return paired_fields(key)[1].astype(jnp.bfloat16)


def level_of(own_key, dims, cuts, low, high):
    gain = 1.0
    for position, blocks in cuts:
        heights = jax.random.uniform(jax.random.fold_in(jax.random.fold_in(own_key, 6), position), (blocks,), jnp.float32, low / len(cuts), high / len(cuts))
        gain = gain * jnp.repeat(jnp.exp(heights), dims[position] // blocks).reshape((-1,) + (1,) * (len(dims) - 1 - position))
    return gain


def assign_block(key, own, number, rows, count, top, bound, slope):
    sequence = jax.random.permutation(key, count)
    crowded, common = shares(count, rows * top, bound, slope, True), shares(count, rows * top, bound, slope, False)
    places = jnp.arange(count)

    def named(tallies, offset_by):
        used = int((tallies > 0).sum())
        fixed = max(1, used // 4)
        passed = fixed + (places - fixed + offset_by * (used - fixed)) % max(1, count - fixed)
        return jnp.zeros((count,), jnp.int32).at[sequence[jnp.where(places < fixed, places, passed)]].set(jnp.asarray(tallies, jnp.int32))

    tallies = jnp.where(number % 4 == 0, named(crowded, number // 4), named(common, number - number // 4 - 1))
    mixed = jax.random.permutation(jax.random.fold_in(own, 3), count)
    source_of, sink = mixed[0:count // 2 * 2:2], mixed[1:count // 2 * 2:2]
    room = jnp.minimum(tallies[source_of] - 1, bound - tallies[sink]) // 2
    room = jnp.where((source_of == sequence[0]) | (sink == sequence[0]) | (tallies[sink] == 0), 0, jnp.maximum(room, 0))
    passed = jax.random.randint(jax.random.fold_in(own, 4), (count // 2,), 0, 1 << 20) % (room + 1)
    tallies = tallies.at[source_of].add(-passed).at[sink].add(passed)
    items = jnp.searchsorted(jnp.cumsum(tallies), jnp.arange(rows * top), side="right").astype(jnp.int32)
    table = items.reshape(top, rows).T
    table = table[jax.random.permutation(jax.random.fold_in(own, 1), rows)]
    offset_by = jax.random.randint(jax.random.fold_in(own, 2), (rows, 1), 0, top)
    return jnp.take_along_axis(table, (jnp.arange(top)[None, :] + offset_by) % top, axis=1)


def shares(count, total, limit, slope, full):
    portions = [(1 << 20) // math.isqrt(standing ** slope) + 1 for standing in range(1, count + 1)]
    largest = limit if full else min(limit, max(-(-total // count), total * portions[0] // sum(portions)))
    least = 1 if total - largest >= count - 1 else 0
    counts, rest = [largest] + [least] * (count - 1), total - largest - least * (count - 1)
    while rest > 0:
        movable = [i for i in range(1, count) if counts[i] < largest] or [i for i in range(1, count) if counts[i] < limit]
        whole, remaining = sum([portions[i] for i in movable]), rest
        for i in movable:
            more = min(limit - counts[i], max(1, remaining * portions[i] // whole), rest)
            counts[i] = counts[i] + more
            rest = rest - more
    return np.array(counts)


def scatter_about(own_key, extent, spread, most, cuts=(), kind=jnp.bfloat16):
    values = spread * jax.random.normal(own_key, extent, jnp.float32)
    if cuts:
        values = values * level_of(own_key, extent, cuts, -0.22, 0.18)
    return jnp.clip(values, -most, most).astype(kind)


def setup_inputs(seed: int = 0, part: int = 0) -> dict:
    key_list = jax.random.split(jax.random.key(seed), 6)
    part_splits = jax.random.split(jax.random.fold_in(key_list[5], part), 6)
    queries = draw_queries(jax.random.fold_in(jax.random.fold_in(key_list[5], part), 71), part)
    keys = draw_keys(jax.random.fold_in(jax.random.fold_in(key_list[5], part), 71), part)
    values = scatter_about(part_splits[2], (TOKENS, H * HD), 1.0, 6.0, ((0, 16),))
    grad_out = scatter_about(part_splits[3], (TOKENS, H * HD), 1.0, 6.0, ((0, 16),))
    partners_keys = jax.random.split(jax.random.fold_in(part_splits[4], 1), BLOCKS * H // H)
    partners_turns = jax.random.permutation(jax.random.fold_in(part_splits[4], 3), BLOCKS * H // H)
    partners = jax.vmap(lambda own, number: assign_block(jax.random.fold_in(part_splits[4], 2), own, number, H, BLOCKS, 3, MOST, 2))(partners_keys, partners_turns).reshape((BLOCKS, H, 3))
    return {"queries": queries, "keys": keys, "values": values, "grad_out": grad_out, "partners": partners}


def rounded(values_f32):
    return lax.optimization_barrier(values_f32.astype(jnp.bfloat16)).astype(jnp.float32)

def reference(queries, keys, values, grad_out, partners):
    block_count = BLOCKS
    width = H * HD
    softmax_scale = 1.0 / math.sqrt(HD)
    query_blocks = queries.reshape(block_count, BLK, H, HD)
    grad_blocks = grad_out.reshape(block_count, BLK, H, HD)
    key_heads = keys.reshape(block_count, BLK, H, HD).transpose(0, 2, 1, 3)
    value_heads = values.reshape(block_count, BLK, H, HD).transpose(0, 2, 1, 3)
    head_ids = jnp.arange(H, dtype=jnp.int32)
    far_slots = jnp.arange(8, dtype=jnp.int32) >= 5

    def step(carry, block_id):
        key_sum, value_sum = carry
        window_ids = jnp.stack([block_id - 1, block_id, block_id + 1]).astype(jnp.int32)
        window_ok = (window_ids >= 0) & (window_ids < block_count)
        clamped = jnp.clip(window_ids, 0, block_count - 1).astype(jnp.int32)
        near_ids = jnp.concatenate([clamped, jnp.array([0, 1], dtype=jnp.int32)])
        targets = jnp.concatenate([jnp.broadcast_to(near_ids[None, :], (H, 5)), partners[block_id].astype(jnp.int32)], axis=1)
        slot_keys = key_heads[targets, head_ids[:, None]].astype(jnp.float32).reshape(H, 8 * BLK, HD)
        slot_values = value_heads[targets, head_ids[:, None]].astype(jnp.float32).reshape(H, 8 * BLK, HD)
        query_rows = query_blocks[block_id].astype(jnp.float32).transpose(1, 0, 2)
        grad_rows = grad_blocks[block_id].astype(jnp.float32).transpose(1, 0, 2)
        scores = jnp.einsum('htd,hkd->htk', query_rows, slot_keys) * softmax_scale
        key_ok = jnp.repeat(jnp.concatenate([window_ok, jnp.ones((5,), dtype=bool)]), BLK)
        masked = jnp.where(key_ok[None, None, :], scores, -jnp.inf)
        row_max = lax.optimization_barrier(jnp.max(masked, axis=2, keepdims=True))
        powers = jnp.exp(masked - row_max)
        probs = powers / lax.optimization_barrier(jnp.sum(powers, axis=2, keepdims=True))
        probs_b = rounded(probs)
        attended = jnp.einsum('htk,hkd->htd', probs_b, slot_values)
        delta = lax.optimization_barrier(jnp.sum(grad_rows * attended, axis=2))
        dprob = jnp.einsum('htd,hkd->htk', grad_rows, slot_values)
        dscore_b = rounded(probs * (dprob - delta[:, :, None]))
        grad_q = softmax_scale * jnp.einsum('htk,hkd->htd', dscore_b, slot_keys)
        grad_q = grad_q.transpose(1, 0, 2).reshape(BLK, width).astype(jnp.bfloat16)
        key_term = (softmax_scale * jnp.einsum('htk,htd->hkd', dscore_b, query_rows)).reshape(H, 8, BLK, HD)
        value_term = jnp.einsum('htk,htd->hkd', probs_b, grad_rows).reshape(H, 8, BLK, HD)
        key_term = jnp.where(far_slots[None, :, None, None], rounded(key_term), key_term)
        value_term = jnp.where(far_slots[None, :, None, None], rounded(value_term), value_term)
        key_sum = key_sum.at[targets, head_ids[:, None]].add(key_term)
        value_sum = value_sum.at[targets, head_ids[:, None]].add(value_term)
        return ((key_sum, value_sum), grad_q)
    zeros_acc = jnp.zeros((block_count, H, BLK, HD), dtype=jnp.float32)
    (key_sum, value_sum), grad_q = lax.scan(step, (zeros_acc, zeros_acc), jnp.arange(block_count, dtype=jnp.int32))
    grad_queries = grad_q.reshape(block_count * BLK, width)
    grad_keys = key_sum.transpose(0, 2, 1, 3).reshape(block_count * BLK, width).astype(jnp.bfloat16)
    grad_values = value_sum.transpose(0, 2, 1, 3).reshape(block_count * BLK, width).astype(jnp.bfloat16)
    return (grad_queries, grad_keys, grad_values)
```

```python
import functools
import math

import jax
import jax.numpy as jnp
from jax import lax
from jax.experimental import pallas as pl
from jax.experimental.pallas import tpu as pltpu
from jax.sharding import PartitionSpec as P

H = 16
HD = 128
BLK = 128
WIDTH = H * HD
SCALE = 1.0 / math.sqrt(HD)
STRIDE = 4
CHUNKS = 8
ROWS = 2 * BLK // CHUNKS
ANY = pl.BlockSpec(memory_space=pl.ANY)
VMEM = pl.BlockSpec(memory_space=pltpu.VMEM)
SMEM = pl.BlockSpec(memory_space=pltpu.SMEM)


def remote(src, dst, send, recv, target):
    return pltpu.make_async_remote_copy(
        src_ref=src, dst_ref=dst, send_sem=send, recv_sem=recv,
        device_id={"seq": target}, device_id_type=pl.DeviceIdType.MESH,
    )


def relations(n):
    me = lax.axis_index("seq")
    return dict(
        me=me,
        core=lax.rem(me, 2),
        sibling=me + 1 - 2 * lax.rem(me, 2),
        lower=me > 0,
        upper=me < n - 1,
        root=me < 2,
        side=jnp.logical_and(me >= 2, me < 4),
        down=me >= STRIDE,
        up=me + STRIDE < n,
    )


def greet(r):
    me = r["me"]
    barrier = pltpu.get_barrier_semaphore()
    peers = ((r["lower"], -1), (r["upper"], 1), (r["down"], -STRIDE), (r["up"], STRIDE), (r["root"], 2), (r["side"], -2))
    for ok, step in peers:
        @pl.when(ok)
        def _(step=step):
            pl.semaphore_signal(barrier, inc=1, device_id={"seq": me + step}, device_id_type=pl.DeviceIdType.MESH)
    pl.semaphore_wait(barrier, sum(ok.astype(jnp.int32) for ok, _ in peers))


def piece(ref, lead, i):
    return ref.at[lead, i // (CHUNKS // 2), pl.ds((i % (CHUNKS // 2)) * ROWS, ROWS)]


def spread_kernel(n, keys, values, near, local, tree_s, tree_r, side_s, sib_s, sib_r, halo_s, halo_r):
    r = relations(n)
    me, core = r["me"], r["core"]
    greet(r)

    def own(i):
        ref = keys if i < CHUNKS // 2 else values
        return ref.at[pl.ds((i % (CHUNKS // 2)) * ROWS, ROWS)]

    def at_local(i):
        return pltpu.make_async_copy(own(i), piece(near, 2 + core, i), local.at[i])

    def to_up(i):
        return remote(piece(near, 2 + core, i), piece(near, 2 + core, i), tree_s.at[i], tree_r.at[i], me + STRIDE)

    def to_side(i):
        return remote(piece(near, 2 + core, i), piece(near, 2 + core, i), side_s.at[i], tree_r.at[i], me + 2)

    def to_sibling(i):
        return remote(piece(near, 2 + core, i), piece(near, 2 + core, i), sib_s.at[i], sib_r.at[i], r["sibling"])

    def from_sibling(i):
        return remote(piece(near, 3 - core, i), piece(near, 3 - core, i), sib_s.at[i], sib_r.at[i], r["sibling"])

    def to_halo(t, up):
        ref = (keys, values)[t]
        slot = 0 if up else 1
        return remote(ref, near.at[slot, t], halo_s.at[slot, t], halo_r.at[slot, t], me + (1 if up else -1))

    @pl.when(r["root"])
    def _():
        for i in range(CHUNKS):
            at_local(i).start()

    for t in range(2):
        for ok, up in ((r["upper"], True), (r["lower"], False)):
            @pl.when(ok)
            def _(t=t, up=up):
                to_halo(t, up).start()

    for i in range(CHUNKS):
        @pl.when(r["root"])
        def _(i=i):
            at_local(i).wait()

        @pl.when(jnp.logical_not(r["root"]))
        def _(i=i):
            to_up(i).wait_recv()

        @pl.when(r["up"])
        def _(i=i):
            to_up(i).start()

        @pl.when(r["root"])
        def _(i=i):
            to_side(i).start()

        to_sibling(i).start()

    for i in range(CHUNKS):
        from_sibling(i).wait_recv()
        to_sibling(i).wait_send()

        @pl.when(r["up"])
        def _(i=i):
            to_up(i).wait_send()

        @pl.when(r["root"])
        def _(i=i):
            to_side(i).wait_send()

    for t in range(2):
        for ok, up in ((r["upper"], True), (r["lower"], False)):
            @pl.when(ok)
            def _(t=t, up=up):
                to_halo(t, up).wait_send()
        for ok, up in ((r["lower"], True), (r["upper"], False)):
            @pl.when(ok)
            def _(t=t, up=up):
                to_halo(t, up).wait_recv()


def spread(keys, values, n):
    return pl.pallas_call(
        functools.partial(spread_kernel, n),
        out_shape=jax.ShapeDtypeStruct((4, 2, BLK, WIDTH), jnp.bfloat16),
        in_specs=[ANY, ANY],
        out_specs=ANY,
        scratch_shapes=[pltpu.SemaphoreType.DMA((CHUNKS,))] * 6
        + [pltpu.SemaphoreType.DMA((2, 2)), pltpu.SemaphoreType.DMA((2, 2))],
        compiler_params=pltpu.CompilerParams(
            collective_id=0, has_side_effects=True, vmem_limit_bytes=48 << 20),
        cost_estimate=pl.CostEstimate(flops=40_000_000_000, bytes_accessed=8 << 20, transcendentals=0),
        name="spread",
    )(keys, values)


def gather_kernel(n, window, sinks, halo, total, sib_in, tree_in, side_in, tree_out,
                  tree_s, tree_r, side_r, sib_s, sib_r, halo_s, halo_r):
    r = relations(n)
    me, core = r["me"], r["core"]
    greet(r)

    def to_sibling(i):
        return remote(piece(sinks, 1 - core, i), sib_in.at[i], sib_s.at[i], sib_r.at[i], r["sibling"])

    def to_down(i):
        return remote(tree_out.at[i], tree_in.at[i], tree_s.at[i], tree_r.at[i], me - STRIDE)

    def to_side(i):
        return remote(tree_out.at[i], side_in.at[i], tree_s.at[i], side_r.at[i], me - 2)

    def to_halo(t, up):
        return remote(window.at[1 if up else 0, t], halo.at[0 if up else 1, t],
                      halo_s.at[0 if up else 1, t], halo_r.at[0 if up else 1, t], me + (1 if up else -1))

    for i in range(CHUNKS):
        to_sibling(i).start()

    for t in range(2):
        for ok, up in ((r["upper"], True), (r["lower"], False)):
            @pl.when(ok)
            def _(t=t, up=up):
                to_halo(t, up).start()

    for i in range(CHUNKS):
        t, rows = i // (CHUNKS // 2), pl.ds((i % (CHUNKS // 2)) * ROWS, ROWS)
        to_sibling(i).wait_recv()
        total[t, rows] = sinks[core, t, rows].astype(jnp.float32) + sib_in[i].astype(jnp.float32)

        @pl.when(r["up"])
        def _(i=i, t=t, rows=rows):
            to_down(i).wait_recv()
            total[t, rows] += tree_in[i].astype(jnp.float32)

        @pl.when(r["root"])
        def _(i=i, t=t, rows=rows):
            to_side(i).wait_recv()
            total[t, rows] += side_in[i].astype(jnp.float32)

        @pl.when(jnp.logical_not(r["root"]))
        def _(i=i, t=t, rows=rows):
            tree_out[i] = total[t, rows].astype(jnp.bfloat16)

        @pl.when(r["down"])
        def _(i=i):
            to_down(i).start()

        @pl.when(r["side"])
        def _(i=i):
            to_side(i).start()

    for i in range(CHUNKS):
        to_sibling(i).wait_send()

        @pl.when(r["down"])
        def _(i=i):
            to_down(i).wait_send()

        @pl.when(r["side"])
        def _(i=i):
            to_side(i).wait_send()

    for t in range(2):
        for ok, up in ((r["upper"], True), (r["lower"], False)):
            @pl.when(ok)
            def _(t=t, up=up):
                to_halo(t, up).wait_send()
        for ok, up in ((r["lower"], True), (r["upper"], False)):
            @pl.when(ok)
            def _(t=t, up=up):
                to_halo(t, up).wait_recv()


def gather(window, sinks, n):
    part = pltpu.VMEM((CHUNKS, ROWS, WIDTH), jnp.bfloat16)
    return pl.pallas_call(
        functools.partial(gather_kernel, n),
        out_shape=(
            jax.ShapeDtypeStruct((2, 2, BLK, WIDTH), jnp.bfloat16),
            jax.ShapeDtypeStruct((2, BLK, WIDTH), jnp.float32),
        ),
        in_specs=[ANY, VMEM],
        out_specs=(ANY, VMEM),
        scratch_shapes=[part] * 4 + [pltpu.SemaphoreType.DMA((CHUNKS,))] * 5
        + [pltpu.SemaphoreType.DMA((2, 2)), pltpu.SemaphoreType.DMA((2, 2))],
        compiler_params=pltpu.CompilerParams(
            collective_id=1, has_side_effects=True, vmem_limit_bytes=48 << 20),
        cost_estimate=pl.CostEstimate(flops=40_000_000_000, bytes_accessed=8 << 20, transcendentals=0),
        name="gather_terms",
    )(window, sinks)


def pick_kernel(count, most, wanted, keys, values, outbox, sem):
    def body(i, _):
        h = jnp.maximum(wanted[i], 0)
        cols = pl.ds(pl.multiple_of(h * HD, HD), HD)
        d, k = i // most, lax.rem(i, most)
        pltpu.make_async_copy(keys.at[:, cols], outbox.at[d, k, 0], sem).start()
        pltpu.make_async_copy(values.at[:, cols], outbox.at[d, k, 1], sem).start()
        return 0

    lax.fori_loop(0, count, body, 0)
    pltpu.make_async_copy(outbox, outbox, sem).wait()


def pick(wanted, keys, values, n, most):
    return pl.pallas_call(
        functools.partial(pick_kernel, n * most, most),
        out_shape=jax.ShapeDtypeStruct((n, most, 2, BLK, HD), jnp.bfloat16),
        in_specs=[SMEM, ANY, ANY],
        out_specs=ANY,
        scratch_shapes=[pltpu.SemaphoreType.DMA],
        cost_estimate=pl.CostEstimate(flops=0, bytes_accessed=6 << 20, transcendentals=0),
        name="pick",
    )(wanted.reshape(-1), keys, values)


def dot(a, b, da, db):
    return lax.dot_general(a, b, (((da,), (db,)), ((), ())), preferred_element_type=jnp.float32)


def core_kernel(n, where, q_ref, g_ref, k_ref, v_ref, near, far0, far1, far2,
                gq_ref, own_ref, window_ref, sink_ref, outbox, terms, sem):
    h = pl.program_id(0)
    slot = lax.rem(h, 2)
    me = where[6 * H]
    lower, upper = me > 0, me < n - 1
    q, g = q_ref[...], g_ref[...]
    zero = jnp.zeros((BLK, HD), jnp.bfloat16)

    def sends(s, hh):
        return [
            pltpu.make_async_copy(
                terms.at[s, j], outbox.at[where[3 * hh + j], where[3 * H + 3 * hh + j]], sem.at[s, j])
            for j in range(3)
        ]

    ks, vs = [], []
    for t, out in ((0, ks), (1, vs)):
        out.append(jnp.where(lower, near[0, t], zero))
        out.append((k_ref, v_ref)[t][...])
        out.append(jnp.where(upper, near[1, t], zero))
        out.append(near[2, t])
        out.append(near[3, t])
        out += [f[0, 0, t] for f in (far0, far1, far2)]
    kc = jnp.concatenate(ks, axis=0)
    vc = jnp.concatenate(vs, axis=0)
    s = dot(kc, q, 1, 1) * SCALE
    row = lax.broadcasted_iota(jnp.int32, (8 * BLK, BLK), 0)
    first = jnp.where(lower, 0, BLK)
    skip = jnp.where(upper, 8 * BLK, 2 * BLK)
    ok = (row >= first) & ((row < skip) | (row >= 3 * BLK))
    s = jnp.where(ok, s, -jnp.inf)
    m = jnp.max(s, axis=0, keepdims=True)
    e = jnp.exp(s - m)
    p = e * (1.0 / jnp.sum(e, axis=0, keepdims=True))
    pb = p.astype(jnp.bfloat16)
    dp = dot(vc, g, 1, 1)
    delta = jnp.sum(pb.astype(jnp.float32) * dp, axis=0, keepdims=True)
    ds = (p * (dp - delta)).astype(jnp.bfloat16)
    gq_ref[...] = (dot(ds, kc, 0, 0) * SCALE).astype(jnp.bfloat16)
    kt = dot(ds, q, 1, 0) * SCALE
    vt = dot(pb, g, 1, 0)

    @pl.when(h >= 2)
    def _():
        for c in sends(slot, h - 2):
            c.wait()

    for t, term in ((0, kt), (1, vt)):
        def at(j, term=term):
            return term[j * BLK:(j + 1) * BLK]

        window_ref[0, t] = at(0).astype(jnp.bfloat16)
        own_ref[0, t] = at(1)
        window_ref[1, t] = at(2).astype(jnp.bfloat16)
        sink_ref[0, t] = at(3).astype(jnp.bfloat16)
        sink_ref[1, t] = at(4).astype(jnp.bfloat16)
        for j in range(3):
            terms[slot, j, t] = at(5 + j).astype(jnp.bfloat16)
    for c in sends(slot, h):
        c.start()

    @pl.when(h == H - 1)
    def _():
        for c in sends(1 - slot, h - 1) + sends(slot, h):
            c.wait()


def attend(where, q, g, k, v, near, fetched, n, most):
    col = pl.BlockSpec((BLK, HD), lambda h, w: (0, h))

    def far(j):
        return pl.BlockSpec(
            (1, 1, 2, BLK, HD), lambda h, w: (w[3 * h + j], w[3 * H + 3 * h + j], 0, 0, 0))

    return pl.pallas_call(
        functools.partial(core_kernel, n),
        out_shape=(
            jax.ShapeDtypeStruct((BLK, WIDTH), jnp.bfloat16),
            jax.ShapeDtypeStruct((H, 2, BLK, HD), jnp.float32),
            jax.ShapeDtypeStruct((2, 2, BLK, WIDTH), jnp.bfloat16),
            jax.ShapeDtypeStruct((2, 2, BLK, WIDTH), jnp.bfloat16),
            jax.ShapeDtypeStruct((n, most, 2, BLK, HD), jnp.bfloat16),
        ),
        grid_spec=pltpu.PrefetchScalarGridSpec(
            num_scalar_prefetch=1,
            grid=(H,),
            in_specs=[col, col, col, col,
                      pl.BlockSpec((4, 2, BLK, HD), lambda h, w: (0, 0, 0, h)),
                      far(0), far(1), far(2)],
            out_specs=(
                col,
                pl.BlockSpec((1, 2, BLK, HD), lambda h, w: (h, 0, 0, 0)),
                pl.BlockSpec((2, 2, BLK, HD), lambda h, w: (0, 0, 0, h)),
                pl.BlockSpec((2, 2, BLK, HD), lambda h, w: (0, 0, 0, h)),
                ANY,
            ),
            scratch_shapes=[
                pltpu.VMEM((2, 3, 2, BLK, HD), jnp.bfloat16),
                pltpu.SemaphoreType.DMA((2, 3)),
            ],
        ),
        compiler_params=pltpu.CompilerParams(vmem_limit_bytes=48 << 20),
        cost_estimate=pl.CostEstimate(flops=3_000_000_000, bytes_accessed=24 << 20, transcendentals=2 << 20),
        name="attend",
    )(where, q, g, k, v, near, fetched, fetched, fetched)


def combine_kernel(n, most, wanted, own, halo, sinks, returned, gk_ref, gv_ref, acc):
    me = wanted[n * most]
    lower, upper, root = me > 0, me < n - 1, me < 2
    for h in range(H):
        cols = slice(h * HD, (h + 1) * HD)
        for t in range(2):
            acc[h, t] = (
                own[h, t]
                + jnp.where(lower, halo[0, t, :, cols].astype(jnp.float32), 0.0)
                + jnp.where(upper, halo[1, t, :, cols].astype(jnp.float32), 0.0)
                + jnp.where(root, sinks[t, :, cols], 0.0)
            )

    def body(i, _):
        h = wanted[i]

        @pl.when(h >= 0)
        def _():
            acc[h] += returned[i].astype(jnp.float32)

        return 0

    lax.fori_loop(0, n * most, body, 0)
    for h in range(H):
        cols = slice(h * HD, (h + 1) * HD)
        gk_ref[:, cols] = acc[h, 0].astype(jnp.bfloat16)
        gv_ref[:, cols] = acc[h, 1].astype(jnp.bfloat16)


def combine(wanted, own, halo, sinks, returned, n, most):
    out = jax.ShapeDtypeStruct((BLK, WIDTH), jnp.bfloat16)
    return pl.pallas_call(
        functools.partial(combine_kernel, n, most),
        out_shape=(out, out),
        in_specs=[SMEM, VMEM, VMEM, VMEM, VMEM],
        out_specs=(VMEM, VMEM),
        scratch_shapes=[pltpu.VMEM((H, 2, BLK, HD), jnp.float32)],
        compiler_params=pltpu.CompilerParams(vmem_limit_bytes=48 << 20),
        cost_estimate=pl.CostEstimate(flops=4_000_000, bytes_accessed=9 << 20, transcendentals=0),
        name="combine",
    )(wanted, own, halo, sinks, returned.reshape(n * most, 2, BLK, HD))


def per_device(queries, keys, values, grad_out, partners):
    n = lax.axis_size("seq")
    me = lax.axis_index("seq").astype(jnp.int32)
    most = max(2, (3 * H + n - 1) // n)
    items = 3 * H
    dests = partners.reshape(items)
    heads = jnp.arange(items, dtype=jnp.int32) // 3
    order = jnp.arange(items)
    same = (dests[:, None] == dests[None, :]) & (order[None, :] < order[:, None])
    rank = jnp.sum(same.astype(jnp.int32), axis=1)
    places = jnp.arange(n * most, dtype=jnp.int32)
    hit = places[:, None] == (dests * most + rank)[None, :]
    requests = jnp.max(jnp.where(hit, heads[None, :], -1), axis=1).reshape(n, most)
    wanted = lax.all_to_all(requests, "seq", split_axis=0, concat_axis=0, tiled=True).reshape(-1)
    picked = pick(wanted, keys, values, n, most)
    fetched = lax.all_to_all(picked, "seq", split_axis=0, concat_axis=0, tiled=True)
    near = spread(keys, values, n)
    where = jnp.concatenate([dests, rank, me[None]])
    grad_queries, own, window, sinks, outbox = attend(
        where, queries, grad_out, keys, values, near, fetched, n, most)
    returned = lax.all_to_all(outbox, "seq", split_axis=0, concat_axis=0, tiled=True)
    halo, total = gather(window, sinks, n)
    table = jnp.concatenate([wanted, me[None]])
    grad_keys, grad_values = combine(table, own, halo, total, returned, n, most)
    return grad_queries, grad_keys, grad_values


def solution(mesh):
    block = P(("groups", "seq"), None)
    return jax.shard_map(
        per_device,
        mesh=mesh,
        in_specs=(block, block, block, block, P(("groups", "seq"), None, None)),
        out_specs=(block, block, block),
        check_vma=False,
    )
```

```python
import functools
import math

import jax
import jax.numpy as jnp
from jax import lax
from jax.experimental import pallas as pl
from jax.experimental.pallas import tpu as pltpu
from jax.sharding import PartitionSpec as P

H = 16
HD = 128
BLK = 128
WIDTH = H * HD
SCALE = 1.0 / math.sqrt(HD)
STRIDE = 4
CHUNKS = 8
ROWS = 2 * BLK // CHUNKS
ANY = pl.BlockSpec(memory_space=pl.ANY)
VMEM = pl.BlockSpec(memory_space=pltpu.VMEM)
SMEM = pl.BlockSpec(memory_space=pltpu.SMEM)


def remote(src, dst, send, recv, target):
    return pltpu.make_async_remote_copy(
        src_ref=src, dst_ref=dst, send_sem=send, recv_sem=recv,
        device_id={"seq": target}, device_id_type=pl.DeviceIdType.MESH,
    )


def relations(n):
    me = lax.axis_index("seq")
    return dict(
        me=me,
        core=lax.rem(me, 2),
        sibling=me + 1 - 2 * lax.rem(me, 2),
        lower=me > 0,
        upper=me < n - 1,
        root=me < 2,
        side=jnp.logical_and(me >= 2, me < 4),
        down=me >= STRIDE,
        up=me + STRIDE < n,
    )


def greet(r):
    me = r["me"]
    barrier = pltpu.get_barrier_semaphore()
    peers = ((r["lower"], -1), (r["upper"], 1), (r["down"], -STRIDE), (r["up"], STRIDE), (r["root"], 2), (r["side"], -2))
    for ok, step in peers:
        @pl.when(ok)
        def _(step=step):
            pl.semaphore_signal(barrier, inc=1, device_id={"seq": me + step}, device_id_type=pl.DeviceIdType.MESH)
    pl.semaphore_wait(barrier, sum(ok.astype(jnp.int32) for ok, _ in peers))


def piece(ref, lead, i):
    return ref.at[lead, i // (CHUNKS // 2), pl.ds((i % (CHUNKS // 2)) * ROWS, ROWS)]


def spread_kernel(n, keys, values, near, local, tree_s, tree_r, side_s, sib_s, sib_r, halo_s, halo_r):
    r = relations(n)
    me, core = r["me"], r["core"]
    greet(r)

    def own(i):
        ref = keys if i < CHUNKS // 2 else values
        return ref.at[pl.ds((i % (CHUNKS // 2)) * ROWS, ROWS)]

    def at_local(i):
        return pltpu.make_async_copy(own(i), piece(near, 2 + core, i), local.at[i])

    def to_up(i):
        return remote(piece(near, 2 + core, i), piece(near, 2 + core, i), tree_s.at[i], tree_r.at[i], me + STRIDE)

    def to_side(i):
        return remote(piece(near, 2 + core, i), piece(near, 2 + core, i), side_s.at[i], tree_r.at[i], me + 2)

    def to_sibling(i):
        return remote(piece(near, 2 + core, i), piece(near, 2 + core, i), sib_s.at[i], sib_r.at[i], r["sibling"])

    def from_sibling(i):
        return remote(piece(near, 3 - core, i), piece(near, 3 - core, i), sib_s.at[i], sib_r.at[i], r["sibling"])

    def to_halo(t, up):
        ref = (keys, values)[t]
        slot = 0 if up else 1
        return remote(ref, near.at[slot, t], halo_s.at[slot, t], halo_r.at[slot, t], me + (1 if up else -1))

    @pl.when(r["root"])
    def _():
        for i in range(CHUNKS):
            at_local(i).start()

    for t in range(2):
        for ok, up in ((r["upper"], True), (r["lower"], False)):
            @pl.when(ok)
            def _(t=t, up=up):
                to_halo(t, up).start()

    for i in range(CHUNKS):
        @pl.when(r["root"])
        def _(i=i):
            at_local(i).wait()

        @pl.when(jnp.logical_not(r["root"]))
        def _(i=i):
            to_up(i).wait_recv()

        @pl.when(r["up"])
        def _(i=i):
            to_up(i).start()

        @pl.when(r["root"])
        def _(i=i):
            to_side(i).start()

        to_sibling(i).start()

    for i in range(CHUNKS):
        from_sibling(i).wait_recv()
        to_sibling(i).wait_send()

        @pl.when(r["up"])
        def _(i=i):
            to_up(i).wait_send()

        @pl.when(r["root"])
        def _(i=i):
            to_side(i).wait_send()

    for t in range(2):
        for ok, up in ((r["upper"], True), (r["lower"], False)):
            @pl.when(ok)
            def _(t=t, up=up):
                to_halo(t, up).wait_send()
        for ok, up in ((r["lower"], True), (r["upper"], False)):
            @pl.when(ok)
            def _(t=t, up=up):
                to_halo(t, up).wait_recv()


def spread(keys, values, n):
    return pl.pallas_call(
        functools.partial(spread_kernel, n),
        out_shape=jax.ShapeDtypeStruct((4, 2, BLK, WIDTH), jnp.bfloat16),
        in_specs=[ANY, ANY],
        out_specs=ANY,
        scratch_shapes=[pltpu.SemaphoreType.DMA((CHUNKS,))] * 6
        + [pltpu.SemaphoreType.DMA((2, 2)), pltpu.SemaphoreType.DMA((2, 2))],
        compiler_params=pltpu.CompilerParams(
            collective_id=0, has_side_effects=True, vmem_limit_bytes=48 << 20),
        cost_estimate=pl.CostEstimate(flops=40_000_000_000, bytes_accessed=8 << 20, transcendentals=0),
        name="spread",
    )(keys, values)


def gather_kernel(n, window, sinks, halo, total, sib_in, tree_in, side_in, tree_out,
                  tree_s, tree_r, side_r, sib_s, sib_r, halo_s, halo_r):
    r = relations(n)
    me, core = r["me"], r["core"]
    greet(r)

    def to_sibling(i):
        return remote(piece(sinks, 1 - core, i), sib_in.at[i], sib_s.at[i], sib_r.at[i], r["sibling"])

    def to_down(i):
        return remote(tree_out.at[i], tree_in.at[i], tree_s.at[i], tree_r.at[i], me - STRIDE)

    def to_side(i):
        return remote(tree_out.at[i], side_in.at[i], tree_s.at[i], side_r.at[i], me - 2)

    def to_halo(t, up):
        return remote(window.at[1 if up else 0, t], halo.at[0 if up else 1, t],
                      halo_s.at[0 if up else 1, t], halo_r.at[0 if up else 1, t], me + (1 if up else -1))

    for i in range(CHUNKS):
        to_sibling(i).start()

    for t in range(2):
        for ok, up in ((r["upper"], True), (r["lower"], False)):
            @pl.when(ok)
            def _(t=t, up=up):
                to_halo(t, up).start()

    for i in range(CHUNKS):
        t, rows = i // (CHUNKS // 2), pl.ds((i % (CHUNKS // 2)) * ROWS, ROWS)
        to_sibling(i).wait_recv()
        total[t, rows] = sinks[core, t, rows].astype(jnp.float32) + sib_in[i].astype(jnp.float32)

        @pl.when(r["up"])
        def _(i=i, t=t, rows=rows):
            to_down(i).wait_recv()
            total[t, rows] += tree_in[i].astype(jnp.float32)

        @pl.when(r["root"])
        def _(i=i, t=t, rows=rows):
            to_side(i).wait_recv()
            total[t, rows] += side_in[i].astype(jnp.float32)

        @pl.when(jnp.logical_not(r["root"]))
        def _(i=i, t=t, rows=rows):
            tree_out[i] = total[t, rows].astype(jnp.bfloat16)

        @pl.when(r["down"])
        def _(i=i):
            to_down(i).start()

        @pl.when(r["side"])
        def _(i=i):
            to_side(i).start()

    for i in range(CHUNKS):
        to_sibling(i).wait_send()

        @pl.when(r["down"])
        def _(i=i):
            to_down(i).wait_send()

        @pl.when(r["side"])
        def _(i=i):
            to_side(i).wait_send()

    for t in range(2):
        for ok, up in ((r["upper"], True), (r["lower"], False)):
            @pl.when(ok)
            def _(t=t, up=up):
                to_halo(t, up).wait_send()
        for ok, up in ((r["lower"], True), (r["upper"], False)):
            @pl.when(ok)
            def _(t=t, up=up):
                to_halo(t, up).wait_recv()


def gather(window, sinks, n):
    part = pltpu.VMEM((CHUNKS, ROWS, WIDTH), jnp.bfloat16)
    return pl.pallas_call(
        functools.partial(gather_kernel, n),
        out_shape=(
            jax.ShapeDtypeStruct((2, 2, BLK, WIDTH), jnp.bfloat16),
            jax.ShapeDtypeStruct((2, BLK, WIDTH), jnp.float32),
        ),
        in_specs=[ANY, VMEM],
        out_specs=(ANY, VMEM),
        scratch_shapes=[part] * 4 + [pltpu.SemaphoreType.DMA((CHUNKS,))] * 5
        + [pltpu.SemaphoreType.DMA((2, 2)), pltpu.SemaphoreType.DMA((2, 2))],
        compiler_params=pltpu.CompilerParams(
            collective_id=1, has_side_effects=True, vmem_limit_bytes=48 << 20),
        cost_estimate=pl.CostEstimate(flops=40_000_000_000, bytes_accessed=8 << 20, transcendentals=0),
        name="gather_terms",
    )(window, sinks)


def pick_kernel(count, most, wanted, keys, values, outbox, held, sem_in, sem):
    loads = []
    for h in range(H):
        cols = pl.ds(h * HD, HD)
        loads.append(pltpu.make_async_copy(keys.at[:, cols], held.at[h, 0], sem_in.at[h, 0]))
        loads.append(pltpu.make_async_copy(values.at[:, cols], held.at[h, 1], sem_in.at[h, 1]))
    for c in loads:
        c.start()
    for c in loads:
        c.wait()

    def body(i, _):
        h = jnp.maximum(wanted[i], 0)
        pltpu.make_async_copy(held.at[h], outbox.at[i // most, lax.rem(i, most)], sem).start()
        return 0

    lax.fori_loop(0, count, body, 0)
    pltpu.make_async_copy(outbox, outbox, sem).wait()


def pick(wanted, keys, values, n, most):
    return pl.pallas_call(
        functools.partial(pick_kernel, n * most, most),
        out_shape=jax.ShapeDtypeStruct((n, most, 2, BLK, HD), jnp.bfloat16),
        in_specs=[SMEM, ANY, ANY],
        out_specs=ANY,
        scratch_shapes=[pltpu.VMEM((H, 2, BLK, HD), jnp.bfloat16),
                        pltpu.SemaphoreType.DMA((H, 2)), pltpu.SemaphoreType.DMA],
        cost_estimate=pl.CostEstimate(flops=0, bytes_accessed=6 << 20, transcendentals=0),
        compiler_params=pltpu.CompilerParams(vmem_limit_bytes=48 << 20),
        name="pick",
    )(wanted.reshape(-1), keys, values)


def dot(a, b, da, db):
    return lax.dot_general(a, b, (((da,), (db,)), ((), ())), preferred_element_type=jnp.float32)


def core_kernel(n, where, q_ref, g_ref, k_ref, v_ref, near, far0, far1, far2,
                gq_ref, own_ref, window_ref, sink_ref, outbox, terms, sem):
    h = pl.program_id(0)
    slot = lax.rem(h, 2)
    me = where[6 * H]
    lower, upper = me > 0, me < n - 1
    q, g = q_ref[...], g_ref[...]
    zero = jnp.zeros((BLK, HD), jnp.bfloat16)

    def sends(s, hh):
        return [
            pltpu.make_async_copy(
                terms.at[s, j], outbox.at[where[3 * hh + j], where[3 * H + 3 * hh + j]], sem.at[s, j])
            for j in range(3)
        ]

    ks, vs = [], []
    for t, out in ((0, ks), (1, vs)):
        out.append(jnp.where(lower, near[0, t], zero))
        out.append((k_ref, v_ref)[t][...])
        out.append(jnp.where(upper, near[1, t], zero))
        out.append(near[2, t])
        out.append(near[3, t])
        out += [f[0, 0, t] for f in (far0, far1, far2)]
    kc = jnp.concatenate(ks, axis=0)
    vc = jnp.concatenate(vs, axis=0)
    s = dot(kc, q, 1, 1) * SCALE
    row = lax.broadcasted_iota(jnp.int32, (8 * BLK, BLK), 0)
    first = jnp.where(lower, 0, BLK)
    skip = jnp.where(upper, 8 * BLK, 2 * BLK)
    ok = (row >= first) & ((row < skip) | (row >= 3 * BLK))
    s = jnp.where(ok, s, -jnp.inf)
    m = jnp.max(s, axis=0, keepdims=True)
    e = jnp.exp(s - m)
    p = e * (1.0 / jnp.sum(e, axis=0, keepdims=True))
    pb = p.astype(jnp.bfloat16)
    dp = dot(vc, g, 1, 1)
    delta = jnp.sum(pb.astype(jnp.float32) * dp, axis=0, keepdims=True)
    ds = (p * (dp - delta)).astype(jnp.bfloat16)
    gq_ref[...] = (dot(ds, kc, 0, 0) * SCALE).astype(jnp.bfloat16)
    kt = dot(ds, q, 1, 0) * SCALE
    vt = dot(pb, g, 1, 0)

    @pl.when(h >= 2)
    def _():
        for c in sends(slot, h - 2):
            c.wait()

    for t, term in ((0, kt), (1, vt)):
        def at(j, term=term):
            return term[j * BLK:(j + 1) * BLK]

        window_ref[0, t] = at(0).astype(jnp.bfloat16)
        own_ref[0, t] = at(1)
        window_ref[1, t] = at(2).astype(jnp.bfloat16)
        sink_ref[0, t] = at(3).astype(jnp.bfloat16)
        sink_ref[1, t] = at(4).astype(jnp.bfloat16)
        for j in range(3):
            terms[slot, j, t] = at(5 + j).astype(jnp.bfloat16)
    for c in sends(slot, h):
        c.start()

    @pl.when(h == H - 1)
    def _():
        for c in sends(1 - slot, h - 1) + sends(slot, h):
            c.wait()


def attend(where, q, g, k, v, near, fetched, n, most):
    col = pl.BlockSpec((BLK, HD), lambda h, w: (0, h))

    def far(j):
        return pl.BlockSpec(
            (1, 1, 2, BLK, HD), lambda h, w: (w[3 * h + j], w[3 * H + 3 * h + j], 0, 0, 0))

    return pl.pallas_call(
        functools.partial(core_kernel, n),
        out_shape=(
            jax.ShapeDtypeStruct((BLK, WIDTH), jnp.bfloat16),
            jax.ShapeDtypeStruct((H, 2, BLK, HD), jnp.float32),
            jax.ShapeDtypeStruct((2, 2, BLK, WIDTH), jnp.bfloat16),
            jax.ShapeDtypeStruct((2, 2, BLK, WIDTH), jnp.bfloat16),
            jax.ShapeDtypeStruct((n, most, 2, BLK, HD), jnp.bfloat16),
        ),
        grid_spec=pltpu.PrefetchScalarGridSpec(
            num_scalar_prefetch=1,
            grid=(H,),
            in_specs=[col, col, col, col,
                      pl.BlockSpec((4, 2, BLK, HD), lambda h, w: (0, 0, 0, h)),
                      far(0), far(1), far(2)],
            out_specs=(
                col,
                pl.BlockSpec((1, 2, BLK, HD), lambda h, w: (h, 0, 0, 0)),
                pl.BlockSpec((2, 2, BLK, HD), lambda h, w: (0, 0, 0, h)),
                pl.BlockSpec((2, 2, BLK, HD), lambda h, w: (0, 0, 0, h)),
                ANY,
            ),
            scratch_shapes=[
                pltpu.VMEM((2, 3, 2, BLK, HD), jnp.bfloat16),
                pltpu.SemaphoreType.DMA((2, 3)),
            ],
        ),
        compiler_params=pltpu.CompilerParams(vmem_limit_bytes=48 << 20),
        cost_estimate=pl.CostEstimate(flops=3_000_000_000, bytes_accessed=24 << 20, transcendentals=2 << 20),
        name="attend",
    )(where, q, g, k, v, near, fetched, fetched, fetched)


def combine_kernel(n, most, wanted, own, halo, sinks, returned, gk_ref, gv_ref, acc):
    me = wanted[n * most]
    lower, upper, root = me > 0, me < n - 1, me < 2
    for h in range(H):
        cols = slice(h * HD, (h + 1) * HD)
        for t in range(2):
            acc[h, t] = (
                own[h, t]
                + jnp.where(lower, halo[0, t, :, cols].astype(jnp.float32), 0.0)
                + jnp.where(upper, halo[1, t, :, cols].astype(jnp.float32), 0.0)
                + jnp.where(root, sinks[t, :, cols], 0.0)
            )

    def body(i, _):
        h = wanted[i]

        @pl.when(h >= 0)
        def _():
            acc[h] += returned[i].astype(jnp.float32)

        return 0

    lax.fori_loop(0, n * most, body, 0)
    for h in range(H):
        cols = slice(h * HD, (h + 1) * HD)
        gk_ref[:, cols] = acc[h, 0].astype(jnp.bfloat16)
        gv_ref[:, cols] = acc[h, 1].astype(jnp.bfloat16)


def combine(wanted, own, halo, sinks, returned, n, most):
    out = jax.ShapeDtypeStruct((BLK, WIDTH), jnp.bfloat16)
    return pl.pallas_call(
        functools.partial(combine_kernel, n, most),
        out_shape=(out, out),
        in_specs=[SMEM, VMEM, VMEM, VMEM, VMEM],
        out_specs=(VMEM, VMEM),
        scratch_shapes=[pltpu.VMEM((H, 2, BLK, HD), jnp.float32)],
        compiler_params=pltpu.CompilerParams(vmem_limit_bytes=48 << 20),
        cost_estimate=pl.CostEstimate(flops=4_000_000, bytes_accessed=9 << 20, transcendentals=0),
        name="combine",
    )(wanted, own, halo, sinks, returned.reshape(n * most, 2, BLK, HD))


def per_device(queries, keys, values, grad_out, partners):
    n = lax.axis_size("seq")
    me = lax.axis_index("seq").astype(jnp.int32)
    most = max(2, (3 * H + n - 1) // n)
    items = 3 * H
    dests = partners.reshape(items)
    heads = jnp.arange(items, dtype=jnp.int32) // 3
    order = jnp.arange(items)
    same = (dests[:, None] == dests[None, :]) & (order[None, :] < order[:, None])
    rank = jnp.sum(same.astype(jnp.int32), axis=1)
    places = jnp.arange(n * most, dtype=jnp.int32)
    hit = places[:, None] == (dests * most + rank)[None, :]
    requests = jnp.max(jnp.where(hit, heads[None, :], -1), axis=1).reshape(n, most)
    wanted = lax.all_to_all(requests, "seq", split_axis=0, concat_axis=0, tiled=True).reshape(-1)
    picked = pick(wanted, keys, values, n, most)
    fetched = lax.all_to_all(picked, "seq", split_axis=0, concat_axis=0, tiled=True)
    near = spread(keys, values, n)
    where = jnp.concatenate([dests, rank, me[None]])
    grad_queries, own, window, sinks, outbox = attend(
        where, queries, grad_out, keys, values, near, fetched, n, most)
    returned = lax.all_to_all(outbox, "seq", split_axis=0, concat_axis=0, tiled=True)
    halo, total = gather(window, sinks, n)
    table = jnp.concatenate([wanted, me[None]])
    grad_keys, grad_values = combine(table, own, halo, total, returned, n, most)
    return grad_queries, grad_keys, grad_values


def solution(mesh):
    block = P(("groups", "seq"), None)
    return jax.shard_map(
        per_device,
        mesh=mesh,
        in_specs=(block, block, block, block, P(("groups", "seq"), None, None)),
        out_specs=(block, block, block),
        check_vma=False,
    )
```

```python
import functools
import math

import jax
import jax.numpy as jnp
from jax import lax
from jax.experimental import pallas as pl
from jax.experimental.pallas import tpu as pltpu
from jax.sharding import PartitionSpec as P

H = 16
HD = 128
BLK = 128
WIDTH = H * HD
SCALE = 1.0 / math.sqrt(HD)
STRIDE = 4
CHUNKS = 4
WINDOW = 3
ROWS = 2 * BLK // CHUNKS
ANY = pl.BlockSpec(memory_space=pl.ANY)
VMEM = pl.BlockSpec(memory_space=pltpu.VMEM)
SMEM = pl.BlockSpec(memory_space=pltpu.SMEM)


def remote(src, dst, send, recv, target):
    return pltpu.make_async_remote_copy(
        src_ref=src, dst_ref=dst, send_sem=send, recv_sem=recv,
        device_id={"seq": target}, device_id_type=pl.DeviceIdType.MESH,
    )


def signs(n):
    me = lax.axis_index("seq")
    rung = me // STRIDE
    root, side = me < 2, jnp.logical_and(me >= 2, me < STRIDE)
    return dict(
        me=me,
        core=lax.rem(me, 2),
        sibling=me + 1 - 2 * lax.rem(me, 2),
        lower=me > 0,
        upper=me < n - 1,
        odd=lax.rem(me, 2) == 1,
        even=lax.rem(me, 2) == 0,
        root=root,
        side=side,
        down=me >= STRIDE,
        up=me + STRIDE < n,
        depth=rung + lax.rem(me, STRIDE) // 2,
        height=n // STRIDE - 1 - rung + root.astype(jnp.int32),
    )


def greet(n):
    me = lax.axis_index("seq")
    barrier = pltpu.get_barrier_semaphore()

    def hail(k, _):
        pl.semaphore_signal(barrier, inc=1, device_id={"seq": lax.rem(me + k, n)},
                            device_id_type=pl.DeviceIdType.MESH)
        return 0

    lax.fori_loop(1, n, hail, 0)
    pl.semaphore_wait(barrier, n - 1)


def offsets(n):
    wide = sorted(range(1, n), key=lambda k: (abs(k - n // 2), k))
    out = []
    while wide:
        out.append(wide.pop(0))
        if wide:
            out.append(wide.pop())
    return out


def piece(ref, lead, i):
    half = CHUNKS // 2
    return ref.at[lead, i // half, pl.ds(pl.multiple_of(lax.rem(i, half) * ROWS, ROWS), ROWS)]


def halo_starts(r, step, to_halo):
    early = ((r["even"], True), (r["odd"], False))
    late = ((jnp.logical_and(r["odd"], r["upper"]), True), (jnp.logical_and(r["even"], r["lower"]), False))
    for t in range(2):
        for sides, at in ((early, 0), (late, (3, 8)[t])):
            if step != at:
                continue
            for ok, up in sides:
                @pl.when(ok)
                def _(t=t, up=up):
                    to_halo(t, up).start()


def halo_waits(r, to_halo):
    for t in range(2):
        for ok, up in ((r["upper"], True), (r["lower"], False)):
            @pl.when(ok)
            def _(t=t, up=up):
                to_halo(t, up).wait_send()
        for ok, up in ((r["lower"], True), (r["upper"], False)):
            @pl.when(ok)
            def _(t=t, up=up):
                to_halo(t, up).wait_recv()


def fetch_kernel(n, most, asks, keys, values, near, fetched, wanted, held, ready, picks,
                 load, ask_s, ask_r, table, all_s, all_r, tree_s, tree_r, side_s, sib_s, sib_r,
                 halo_s, halo_r):
    r = signs(n)
    me, core, root = r["me"], r["core"], r["root"]
    loads = []
    for h in range(H):
        cols = pl.ds(h * HD, HD)
        loads.append(pltpu.make_async_copy(keys.at[:, cols], held.at[h, 0], load.at[h, 0]))
        loads.append(pltpu.make_async_copy(values.at[:, cols], held.at[h, 1], load.at[h, 1]))
    for c in loads:
        c.start()
    greet(n)

    def ask(k):
        peer = lax.rem(me + k, n)
        return remote(asks.at[peer], wanted.at[me], ask_s.at[peer], ask_r.at[me], peer)

    def asked(k):
        peer = lax.rem(me + k, n)
        return remote(asks.at[peer], wanted.at[peer], ask_s.at[peer], ask_r.at[peer], peer)

    for k in range(1, n):
        ask(k).start()
    mine = pltpu.make_async_copy(asks.at[me], wanted.at[me], table)
    mine.start()

    def own(t, i):
        return (keys, values)[t].at[pl.ds(pl.multiple_of(lax.rem(i, CHUNKS // 2) * ROWS, ROWS), ROWS)]

    def to_up(i, src):
        return remote(src, piece(near, 2 + core, i), tree_s.at[i], tree_r.at[i], me + STRIDE)

    def to_side(i, src):
        return remote(src, piece(near, 2 + core, i), side_s.at[i], tree_r.at[i], me + 2)

    def to_sibling(i, src):
        return remote(src, piece(near, 2 + core, i), sib_s.at[i], sib_r.at[i], r["sibling"])

    def from_sibling(i):
        return remote(piece(near, 3 - core, i), piece(near, 3 - core, i), sib_s.at[i], sib_r.at[i], r["sibling"])

    def keep(t):
        return pltpu.make_async_copy((keys, values)[t], near.at[2 + core, t], load.at[t, 0])

    def to_halo(t, up):
        slot = 0 if up else 1
        return remote((keys, values)[t], near.at[slot, t], halo_s.at[slot, t], halo_r.at[slot, t],
                      me + (1 if up else -1))

    def relay(i):
        for t in range(2):
            @pl.when(jnp.logical_and(root, i // (CHUNKS // 2) == t))
            def _(t=t):
                @pl.when(r["up"])
                def _():
                    to_up(i, own(t, i)).start()

                to_side(i, own(t, i)).start()
                to_sibling(i, own(t, i)).start()

        @pl.when(jnp.logical_not(root))
        def _():
            to_up(i, piece(near, 2 + core, i)).wait_recv()

            @pl.when(r["up"])
            def _():
                to_up(i, piece(near, 2 + core, i)).start()

            to_sibling(i, piece(near, 2 + core, i)).start()

    def relay_at(step):
        i = step - 2 * r["depth"]

        @pl.when(jnp.logical_and(i >= 0, i < CHUNKS))
        def _():
            relay(i)

    relay_at(0)
    halo_starts(r, 0, to_halo)
    for c in loads:
        c.wait()

    @pl.when(root)
    def _():
        for t in range(2):
            keep(t).start()

    for k in range(1, n):
        asked(k).wait_recv()
    mine.wait()
    copy = pltpu.make_async_copy(wanted, picks, table)
    copy.start()
    copy.wait()

    def fill(peer):
        for j in range(most):
            ready[peer, j] = held[jnp.maximum(picks[peer, 0, j], 0)]

    def send(k):
        peer = lax.rem(me + k, n)
        return remote(ready.at[peer], fetched.at[me], all_s.at[peer], all_r.at[me], peer)

    def sent(k):
        peer = lax.rem(me + k, n)
        return remote(ready.at[peer], fetched.at[peer], all_s.at[peer], all_r.at[peer], peer)

    hops = offsets(n)
    for step, k in enumerate(hops):
        fill(lax.rem(me + k, n))
        if step >= WINDOW:
            send(hops[step - WINDOW]).wait_send()
        send(k).start()
        if step:
            relay_at(step)
            halo_starts(r, step, to_halo)
    fill(me)
    self_copy = pltpu.make_async_copy(ready.at[me], fetched.at[me], table)
    self_copy.start()
    for k in hops[-WINDOW:]:
        send(k).wait_send()
    for k in hops:
        sent(k).wait_recv()
    for k in range(1, n):
        ask(k).wait_send()
    for i in range(CHUNKS):
        from_sibling(i).wait_recv()
        to_sibling(i, piece(near, 2 + core, i)).wait_send()

        @pl.when(r["up"])
        def _(i=i):
            to_up(i, piece(near, 2 + core, i)).wait_send()

        @pl.when(root)
        def _(i=i):
            to_side(i, piece(near, 2 + core, i)).wait_send()

    @pl.when(root)
    def _():
        for t in range(2):
            keep(t).wait()

    self_copy.wait()
    halo_waits(r, to_halo)


def fetch(asks, keys, values, n, most):
    dma = pltpu.SemaphoreType.DMA
    return pl.pallas_call(
        functools.partial(fetch_kernel, n, most),
        out_shape=(
            jax.ShapeDtypeStruct((4, 2, BLK, WIDTH), jnp.bfloat16),
            jax.ShapeDtypeStruct((n, most, 2, BLK, HD), jnp.bfloat16),
            jax.ShapeDtypeStruct((n, 1, 128), jnp.int32),
        ),
        in_specs=[VMEM, ANY, ANY],
        out_specs=(ANY, ANY, VMEM),
        scratch_shapes=[
            pltpu.VMEM((H, 2, BLK, HD), jnp.bfloat16),
            pltpu.VMEM((n, most, 2, BLK, HD), jnp.bfloat16),
            pltpu.SMEM((n, 1, 128), jnp.int32),
            dma((H, 2)), dma((n,)), dma((n,)), dma, dma((n,)), dma((n,)),
            dma((CHUNKS,)), dma((CHUNKS,)), dma((CHUNKS,)), dma((CHUNKS,)), dma((CHUNKS,)),
            dma((2, 2)), dma((2, 2)),
        ],
        compiler_params=pltpu.CompilerParams(
            collective_id=0, has_side_effects=True, vmem_limit_bytes=48 << 20),
        name="fetch",
    )(asks, keys, values)


def collect_kernel(n, outbox, window, sinks, returned, halo, total, sib_in, tree_in, side_in, tree_out,
                   table, all_s, all_r, tree_s, tree_r, side_r, sib_s, sib_r, halo_s, halo_r):
    r = signs(n)
    me, core = r["me"], r["core"]
    greet(n)

    def to_sibling(i):
        return remote(piece(sinks, 1 - core, i), sib_in.at[i], sib_s.at[i], sib_r.at[i], r["sibling"])

    def to_down(i):
        return remote(tree_out.at[i], tree_in.at[i], tree_s.at[i], tree_r.at[i], me - STRIDE)

    def to_side(i):
        return remote(tree_out.at[i], side_in.at[i], tree_s.at[i], side_r.at[i], me - 2)

    def to_halo(t, up):
        slot = 0 if up else 1
        return remote(window.at[1 - slot, t], halo.at[slot, t],
                      halo_s.at[slot, t], halo_r.at[slot, t], me + (1 if up else -1))

    def send(k):
        peer = lax.rem(me + k, n)
        return remote(outbox.at[peer], returned.at[me], all_s.at[peer], all_r.at[me], peer)

    def sent(k):
        peer = lax.rem(me + k, n)
        return remote(outbox.at[peer], returned.at[peer], all_s.at[peer], all_r.at[peer], peer)

    def add(i):
        half = CHUNKS // 2
        t, rows = i // half, pl.ds(pl.multiple_of(lax.rem(i, half) * ROWS, ROWS), ROWS)
        to_sibling(i).wait_recv()
        total[t, rows] = sinks[core, t, rows].astype(jnp.float32) + sib_in[i].astype(jnp.float32)

        @pl.when(r["up"])
        def _():
            to_down(i).wait_recv()
            total[t, rows] += tree_in[i].astype(jnp.float32)

        @pl.when(r["root"])
        def _():
            to_side(i).wait_recv()
            total[t, rows] += side_in[i].astype(jnp.float32)

        @pl.when(jnp.logical_not(r["root"]))
        def _():
            tree_out[i] = total[t, rows].astype(jnp.bfloat16)

        @pl.when(r["down"])
        def _():
            to_down(i).start()

        @pl.when(r["side"])
        def _():
            to_side(i).start()

    for i in range(CHUNKS):
        to_sibling(i).start()
    hops = offsets(n)
    for step, k in enumerate(hops):
        if step >= WINDOW:
            send(hops[step - WINDOW]).wait_send()
        send(k).start()
        halo_starts(r, step, to_halo)
        i = step - 2 * r["height"] - 1

        @pl.when(jnp.logical_and(i >= 0, i < CHUNKS))
        def _(i=i):
            add(i)

    self_copy = pltpu.make_async_copy(outbox.at[me], returned.at[me], table)
    self_copy.start()
    for k in hops[-WINDOW:]:
        send(k).wait_send()
    for k in hops:
        sent(k).wait_recv()
    for i in range(CHUNKS):
        to_sibling(i).wait_send()

        @pl.when(r["down"])
        def _(i=i):
            to_down(i).wait_send()

        @pl.when(r["side"])
        def _(i=i):
            to_side(i).wait_send()

    self_copy.wait()
    halo_waits(r, to_halo)


def collect(outbox, window, sinks, n, most):
    dma = pltpu.SemaphoreType.DMA
    part = pltpu.VMEM((CHUNKS, ROWS, WIDTH), jnp.bfloat16)
    return pl.pallas_call(
        functools.partial(collect_kernel, n),
        out_shape=(
            jax.ShapeDtypeStruct((n, most, 2, BLK, HD), jnp.bfloat16),
            jax.ShapeDtypeStruct((2, 2, BLK, WIDTH), jnp.bfloat16),
            jax.ShapeDtypeStruct((2, BLK, WIDTH), jnp.float32),
        ),
        in_specs=[ANY, ANY, VMEM],
        out_specs=(ANY, ANY, VMEM),
        scratch_shapes=[part] * 4 + [dma, dma((n,)), dma((n,))] + [dma((CHUNKS,))] * 5 + [dma((2, 2))] * 2,
        compiler_params=pltpu.CompilerParams(
            collective_id=1, has_side_effects=True, vmem_limit_bytes=48 << 20),
        name="collect",
    )(outbox, window, sinks)


def dot(a, b, da, db):
    return lax.dot_general(a, b, (((da,), (db,)), ((), ())), preferred_element_type=jnp.float32)


def core_kernel(n, where, q_ref, g_ref, k_ref, v_ref, near, far0, far1, far2,
                gq_ref, own_ref, window_ref, sink_ref, outbox, terms, sem):
    h = pl.program_id(0)
    slot = lax.rem(h, 2)
    me = where[6 * H]
    lower, upper = me > 0, me < n - 1
    q, g = q_ref[...], g_ref[...]
    zero = jnp.zeros((BLK, HD), jnp.bfloat16)

    def sends(s, hh):
        return [
            pltpu.make_async_copy(
                terms.at[s, j], outbox.at[where[3 * hh + j], where[3 * H + 3 * hh + j]], sem.at[s, j])
            for j in range(3)
        ]

    ks, vs = [], []
    for t, out in ((0, ks), (1, vs)):
        out.append(jnp.where(lower, near[0, t], zero))
        out.append((k_ref, v_ref)[t][...])
        out.append(jnp.where(upper, near[1, t], zero))
        out.append(near[2, t])
        out.append(near[3, t])
        out += [f[0, 0, t] for f in (far0, far1, far2)]
    kc = jnp.concatenate(ks, axis=0)
    vc = jnp.concatenate(vs, axis=0)
    s = dot(kc, q, 1, 1) * SCALE
    row = lax.broadcasted_iota(jnp.int32, (8 * BLK, BLK), 0)
    first = jnp.where(lower, 0, BLK)
    skip = jnp.where(upper, 8 * BLK, 2 * BLK)
    ok = (row >= first) & ((row < skip) | (row >= 3 * BLK))
    s = jnp.where(ok, s, -jnp.inf)
    m = jnp.max(s, axis=0, keepdims=True)
    e = jnp.exp(s - m)
    p = e * (1.0 / jnp.sum(e, axis=0, keepdims=True))
    pb = p.astype(jnp.bfloat16)
    dp = dot(vc, g, 1, 1)
    delta = jnp.sum(pb.astype(jnp.float32) * dp, axis=0, keepdims=True)
    ds = (p * (dp - delta)).astype(jnp.bfloat16)
    gq_ref[...] = (dot(ds, kc, 0, 0) * SCALE).astype(jnp.bfloat16)
    kt = dot(ds, q, 1, 0) * SCALE
    vt = dot(pb, g, 1, 0)

    @pl.when(h >= 2)
    def _():
        for c in sends(slot, h - 2):
            c.wait()

    for t, term in ((0, kt), (1, vt)):
        def at(j, term=term):
            return term[j * BLK:(j + 1) * BLK]

        window_ref[0, t] = at(0).astype(jnp.bfloat16)
        own_ref[0, t] = at(1)
        window_ref[1, t] = at(2).astype(jnp.bfloat16)
        sink_ref[0, t] = at(3).astype(jnp.bfloat16)
        sink_ref[1, t] = at(4).astype(jnp.bfloat16)
        for j in range(3):
            terms[slot, j, t] = at(5 + j).astype(jnp.bfloat16)
    for c in sends(slot, h):
        c.start()

    @pl.when(h == H - 1)
    def _():
        for c in sends(1 - slot, h - 1) + sends(slot, h):
            c.wait()


def attend(where, q, g, k, v, near, fetched, n, most):
    col = pl.BlockSpec((BLK, HD), lambda h, w: (0, h))

    def far(j):
        return pl.BlockSpec(
            (1, 1, 2, BLK, HD), lambda h, w: (w[3 * h + j], w[3 * H + 3 * h + j], 0, 0, 0))

    return pl.pallas_call(
        functools.partial(core_kernel, n),
        out_shape=(
            jax.ShapeDtypeStruct((BLK, WIDTH), jnp.bfloat16),
            jax.ShapeDtypeStruct((H, 2, BLK, HD), jnp.float32),
            jax.ShapeDtypeStruct((2, 2, BLK, WIDTH), jnp.bfloat16),
            jax.ShapeDtypeStruct((2, 2, BLK, WIDTH), jnp.bfloat16),
            jax.ShapeDtypeStruct((n, most, 2, BLK, HD), jnp.bfloat16),
        ),
        grid_spec=pltpu.PrefetchScalarGridSpec(
            num_scalar_prefetch=1,
            grid=(H,),
            in_specs=[col, col, col, col,
                      pl.BlockSpec((4, 2, BLK, HD), lambda h, w: (0, 0, 0, h)),
                      far(0), far(1), far(2)],
            out_specs=(
                col,
                pl.BlockSpec((1, 2, BLK, HD), lambda h, w: (h, 0, 0, 0)),
                pl.BlockSpec((2, 2, BLK, HD), lambda h, w: (0, 0, 0, h)),
                pl.BlockSpec((2, 2, BLK, HD), lambda h, w: (0, 0, 0, h)),
                ANY,
            ),
            scratch_shapes=[
                pltpu.VMEM((2, 3, 2, BLK, HD), jnp.bfloat16),
                pltpu.SemaphoreType.DMA((2, 3)),
            ],
        ),
        compiler_params=pltpu.CompilerParams(vmem_limit_bytes=48 << 20),
        cost_estimate=pl.CostEstimate(flops=3_000_000_000, bytes_accessed=24 << 20, transcendentals=2 << 20),
        name="attend",
    )(where, q, g, k, v, near, fetched, fetched, fetched)


def combine_kernel(n, most, wanted, own, halo, sinks, returned, gk_ref, gv_ref, acc):
    me = wanted[n * most]
    lower, upper, root = me > 0, me < n - 1, me < 2
    for h in range(H):
        cols = slice(h * HD, (h + 1) * HD)
        for t in range(2):
            acc[h, t] = (
                own[h, t]
                + jnp.where(lower, halo[0, t, :, cols].astype(jnp.float32), 0.0)
                + jnp.where(upper, halo[1, t, :, cols].astype(jnp.float32), 0.0)
                + jnp.where(root, sinks[t, :, cols], 0.0)
            )

    def body(i, _):
        h = wanted[i]

        @pl.when(h >= 0)
        def _():
            acc[h] += returned[i].astype(jnp.float32)

        return 0

    lax.fori_loop(0, n * most, body, 0)
    for h in range(H):
        cols = slice(h * HD, (h + 1) * HD)
        gk_ref[:, cols] = acc[h, 0].astype(jnp.bfloat16)
        gv_ref[:, cols] = acc[h, 1].astype(jnp.bfloat16)


def combine(wanted, own, halo, sinks, returned, n, most):
    out = jax.ShapeDtypeStruct((BLK, WIDTH), jnp.bfloat16)
    return pl.pallas_call(
        functools.partial(combine_kernel, n, most),
        out_shape=(out, out),
        in_specs=[SMEM, VMEM, VMEM, VMEM, VMEM],
        out_specs=(VMEM, VMEM),
        scratch_shapes=[pltpu.VMEM((H, 2, BLK, HD), jnp.float32)],
        compiler_params=pltpu.CompilerParams(vmem_limit_bytes=48 << 20),
        cost_estimate=pl.CostEstimate(flops=4_000_000, bytes_accessed=9 << 20, transcendentals=0),
        name="combine",
    )(wanted, own, halo, sinks, returned.reshape(n * most, 2, BLK, HD))


def per_device(queries, keys, values, grad_out, partners):
    n = lax.axis_size("seq")
    me = lax.axis_index("seq").astype(jnp.int32)
    most = max(2, (3 * H + n - 1) // n)
    items = 3 * H
    dests = partners.reshape(items)
    heads = jnp.arange(items, dtype=jnp.int32) // 3
    order = jnp.arange(items)
    same = (dests[:, None] == dests[None, :]) & (order[None, :] < order[:, None])
    rank = jnp.sum(same.astype(jnp.int32), axis=1)
    places = jnp.arange(n * 128, dtype=jnp.int32)
    hit = places[:, None] == (dests * 128 + rank)[None, :]
    asks = jnp.max(jnp.where(hit, heads[None, :], -1), axis=1).reshape(n, 1, 128)
    near, fetched, wanted = fetch(asks, keys, values, n, most)
    where = jnp.concatenate([dests, rank, me[None]])
    grad_queries, own, window, sinks, outbox = attend(
        where, queries, grad_out, keys, values, near, fetched, n, most)
    returned, halo, total = collect(outbox, window, sinks, n, most)
    table = jnp.concatenate([wanted[:, 0, :most].reshape(-1), me[None]])
    grad_keys, grad_values = combine(table, own, halo, total, returned, n, most)
    return grad_queries, grad_keys, grad_values


def solution(mesh):
    block = P(("groups", "seq"), None)
    return jax.shard_map(
        per_device,
        mesh=mesh,
        in_specs=(block, block, block, block, P(("groups", "seq"), None, None)),
        out_specs=(block, block, block),
        check_vma=False,
    )
```

```python
import functools
import math

import jax
import jax.numpy as jnp
from jax import lax
from jax.experimental import pallas as pl
from jax.experimental.pallas import tpu as pltpu
from jax.sharding import PartitionSpec as P

H = 16
HD = 128
BLK = 128
WIDTH = H * HD
SCALE = 1.0 / math.sqrt(HD)
STRIDE = 4
CHUNKS = 4
WINDOW = 6
ROWS = 2 * BLK // CHUNKS
ANY = pl.BlockSpec(memory_space=pl.ANY)
VMEM = pl.BlockSpec(memory_space=pltpu.VMEM)
SMEM = pl.BlockSpec(memory_space=pltpu.SMEM)


def remote(src, dst, send, recv, target):
    return pltpu.make_async_remote_copy(
        src_ref=src, dst_ref=dst, send_sem=send, recv_sem=recv,
        device_id={"seq": target}, device_id_type=pl.DeviceIdType.MESH,
    )


def signs(n):
    me = lax.axis_index("seq")
    rung = me // STRIDE
    root = me < 2
    column = lax.rem(me, STRIDE) // 2
    return dict(
        me=me,
        core=lax.rem(me, 2),
        sibling=me + 1 - 2 * lax.rem(me, 2),
        lower=me > 0,
        upper=me < n - 1,
        odd=lax.rem(me, 2) == 1,
        even=lax.rem(me, 2) == 0,
        root=root,
        high=me >= STRIDE,
        up=me + STRIDE < n,
        rung=rung,
        column=column,
        across=me + 2 - 4 * column,
    )


def greet(n):
    me = lax.axis_index("seq")
    barrier = pltpu.get_barrier_semaphore()

    def hail(k, _):
        pl.semaphore_signal(barrier, inc=1, device_id={"seq": lax.rem(me + k, n)},
                            device_id_type=pl.DeviceIdType.MESH)
        return 0

    lax.fori_loop(1, n, hail, 0)
    pl.semaphore_wait(barrier, n - 1)


def offsets(n):
    wide = sorted(range(1, n), key=lambda k: (abs(k - n // 2), k))
    out = []
    while wide:
        out.append(wide.pop(0))
        if wide:
            out.append(wide.pop())
    return out


def piece(ref, lead, i):
    half = CHUNKS // 2
    return ref.at[lead, i // half, pl.ds(pl.multiple_of(lax.rem(i, half) * ROWS, ROWS), ROWS)]


def halo_starts(r, step, to_halo):
    early = ((r["even"], True), (r["odd"], False))
    late = ((jnp.logical_and(r["odd"], r["upper"]), True), (jnp.logical_and(r["even"], r["lower"]), False))
    for t in range(2):
        for sides, at in ((early, 0), (late, (3, 8)[t])):
            if step != at:
                continue
            for ok, up in sides:
                @pl.when(ok)
                def _(t=t, up=up):
                    to_halo(t, up).start()


def halo_waits(r, to_halo):
    for t in range(2):
        for ok, up in ((r["upper"], True), (r["lower"], False)):
            @pl.when(ok)
            def _(t=t, up=up):
                to_halo(t, up).wait_send()
        for ok, up in ((r["lower"], True), (r["upper"], False)):
            @pl.when(ok)
            def _(t=t, up=up):
                to_halo(t, up).wait_recv()


def fetch_kernel(n, most, asks, keys, values, near, fetched, wanted, held, ready, picks,
                 load, ask_s, ask_r, table, all_s, all_r, tree_s, tree_r, side_s, sib_s, sib_r,
                 halo_s, halo_r):
    r = signs(n)
    me, core, root = r["me"], r["core"], r["root"]
    loads = []
    for h in range(H):
        cols = pl.ds(h * HD, HD)
        loads.append(pltpu.make_async_copy(keys.at[:, cols], held.at[h, 0], load.at[h, 0]))
        loads.append(pltpu.make_async_copy(values.at[:, cols], held.at[h, 1], load.at[h, 1]))
    for c in loads:
        c.start()
    greet(n)

    def ask(k):
        peer = lax.rem(me + k, n)
        return remote(asks.at[peer], wanted.at[me], ask_s.at[peer], ask_r.at[me], peer)

    def asked(k):
        peer = lax.rem(me + k, n)
        return remote(asks.at[peer], wanted.at[peer], ask_s.at[peer], ask_r.at[peer], peer)

    for k in range(1, n):
        ask(k).start()
    mine = pltpu.make_async_copy(asks.at[me], wanted.at[me], table)
    mine.start()

    def own(t, i):
        return (keys, values)[t].at[pl.ds(pl.multiple_of(lax.rem(i, CHUNKS // 2) * ROWS, ROWS), ROWS)]

    def to_up(i, src):
        return remote(src, piece(near, 2 + core, i), tree_s.at[i], tree_r.at[i], me + STRIDE)

    def to_side(i, src):
        return remote(src, piece(near, 2 + core, i), side_s.at[i], tree_r.at[i], r["across"])

    def to_sibling(i, src):
        return remote(src, piece(near, 2 + core, i), sib_s.at[i], sib_r.at[i], r["sibling"])

    def from_sibling(i):
        return remote(piece(near, 3 - core, i), piece(near, 3 - core, i), sib_s.at[i], sib_r.at[i], r["sibling"])

    def keep(t):
        return pltpu.make_async_copy((keys, values)[t], near.at[2 + core, t], load.at[t, 0])

    def to_halo(t, up):
        slot = 0 if up else 1
        return remote((keys, values)[t], near.at[slot, t], halo_s.at[slot, t], halo_r.at[slot, t],
                      me + (1 if up else -1))

    def rises(p):
        return jnp.logical_and(r["up"], r["column"] == p)

    def crosses(p):
        return jnp.logical_or(root, jnp.logical_and(r["high"], r["column"] == p))

    def relay(i, p):
        for t in range(2):
            @pl.when(jnp.logical_and(root, i // (CHUNKS // 2) == t))
            def _(t=t):
                @pl.when(rises(p))
                def _():
                    to_up(i, own(t, i)).start()

                to_side(i, own(t, i)).start()
                to_sibling(i, own(t, i)).start()

        @pl.when(jnp.logical_not(root))
        def _():
            to_up(i, piece(near, 2 + core, i)).wait_recv()

            @pl.when(rises(p))
            def _():
                to_up(i, piece(near, 2 + core, i)).start()

            @pl.when(crosses(p))
            def _():
                to_side(i, piece(near, 2 + core, i)).start()

            to_sibling(i, piece(near, 2 + core, i)).start()

    def relay_at(step):
        for p in range(2):
            lag = 2 * r["rung"] + (2 * r["column"] if p == 0 else 3 - r["column"])
            i = step - jnp.where(root, 0, lag)

            @pl.when(jnp.logical_and(jnp.logical_and(i >= 0, i < CHUNKS), lax.rem(i + 2 * n, 2) == p))
            def _(i=i, p=p):
                relay(i, p)

    relay_at(0)
    halo_starts(r, 0, to_halo)
    for c in loads:
        c.wait()

    @pl.when(root)
    def _():
        for t in range(2):
            keep(t).start()

    for k in range(1, n):
        asked(k).wait_recv()
    mine.wait()
    copy = pltpu.make_async_copy(wanted, picks, table)
    copy.start()
    copy.wait()

    def fill(peer):
        for j in range(most):
            ready[peer, j] = held[jnp.maximum(picks[peer, 0, j], 0)]

    def send(k):
        peer = lax.rem(me + k, n)
        return remote(ready.at[peer], fetched.at[me], all_s.at[peer], all_r.at[me], peer)

    def sent(k):
        peer = lax.rem(me + k, n)
        return remote(ready.at[peer], fetched.at[peer], all_s.at[peer], all_r.at[peer], peer)

    hops = offsets(n)
    for step, k in enumerate(hops):
        fill(lax.rem(me + k, n))
        if step >= WINDOW:
            send(hops[step - WINDOW]).wait_send()
        send(k).start()
        if step:
            relay_at(step)
            halo_starts(r, step, to_halo)
    fill(me)
    self_copy = pltpu.make_async_copy(ready.at[me], fetched.at[me], table)
    self_copy.start()
    for k in hops[-WINDOW:]:
        send(k).wait_send()
    for k in hops:
        sent(k).wait_recv()
    for k in range(1, n):
        ask(k).wait_send()
    for i in range(CHUNKS):
        from_sibling(i).wait_recv()
        to_sibling(i, piece(near, 2 + core, i)).wait_send()

        @pl.when(rises(i % 2))
        def _(i=i):
            to_up(i, piece(near, 2 + core, i)).wait_send()

        @pl.when(crosses(i % 2))
        def _(i=i):
            to_side(i, piece(near, 2 + core, i)).wait_send()

    @pl.when(root)
    def _():
        for t in range(2):
            keep(t).wait()

    self_copy.wait()
    halo_waits(r, to_halo)


def fetch(asks, keys, values, n, most):
    dma = pltpu.SemaphoreType.DMA
    return pl.pallas_call(
        functools.partial(fetch_kernel, n, most),
        out_shape=(
            jax.ShapeDtypeStruct((4, 2, BLK, WIDTH), jnp.bfloat16),
            jax.ShapeDtypeStruct((n, most, 2, BLK, HD), jnp.bfloat16),
            jax.ShapeDtypeStruct((n, 1, 128), jnp.int32),
        ),
        in_specs=[VMEM, ANY, ANY],
        out_specs=(ANY, ANY, VMEM),
        scratch_shapes=[
            pltpu.VMEM((H, 2, BLK, HD), jnp.bfloat16),
            pltpu.VMEM((n, most, 2, BLK, HD), jnp.bfloat16),
            pltpu.SMEM((n, 1, 128), jnp.int32),
            dma((H, 2)), dma((n,)), dma((n,)), dma, dma((n,)), dma((n,)),
            dma((CHUNKS,)), dma((CHUNKS,)), dma((CHUNKS,)), dma((CHUNKS,)), dma((CHUNKS,)),
            dma((2, 2)), dma((2, 2)),
        ],
        compiler_params=pltpu.CompilerParams(
            collective_id=0, has_side_effects=True, vmem_limit_bytes=48 << 20),
        name="fetch",
    )(asks, keys, values)


def collect_kernel(n, outbox, window, sinks, returned, halo, total, sib_in, tree_in, side_in, tree_out,
                   table, all_s, all_r, tree_s, tree_r, side_r, sib_s, sib_r, halo_s, halo_r):
    r = signs(n)
    me, core = r["me"], r["core"]
    greet(n)

    def to_sibling(i):
        return remote(piece(sinks, 1 - core, i), sib_in.at[i], sib_s.at[i], sib_r.at[i], r["sibling"])

    def to_down(i):
        return remote(tree_out.at[i], tree_in.at[i], tree_s.at[i], tree_r.at[i], me - STRIDE)

    def to_side(i):
        return remote(tree_out.at[i], side_in.at[i], tree_s.at[i], side_r.at[i], r["across"])

    def to_halo(t, up):
        slot = 0 if up else 1
        return remote(window.at[1 - slot, t], halo.at[slot, t],
                      halo_s.at[slot, t], halo_r.at[slot, t], me + (1 if up else -1))

    def send(k):
        peer = lax.rem(me + k, n)
        return remote(outbox.at[peer], returned.at[me], all_s.at[peer], all_r.at[me], peer)

    def sent(k):
        peer = lax.rem(me + k, n)
        return remote(outbox.at[peer], returned.at[peer], all_s.at[peer], all_r.at[peer], peer)

    def trunk(p):
        return r["column"] == p

    def falls(p):
        return jnp.logical_and(trunk(p), r["high"])

    def crosses(p):
        return jnp.logical_not(jnp.logical_or(r["root"], falls(p)))

    def add(i, p):
        half = CHUNKS // 2
        t, rows = i // half, pl.ds(pl.multiple_of(lax.rem(i, half) * ROWS, ROWS), ROWS)
        to_sibling(i).wait_recv()
        total[t, rows] = sinks[core, t, rows].astype(jnp.float32) + sib_in[i].astype(jnp.float32)

        @pl.when(jnp.logical_and(r["up"], trunk(p)))
        def _():
            to_down(i).wait_recv()
            total[t, rows] += tree_in[i].astype(jnp.float32)

        @pl.when(jnp.logical_or(r["root"], falls(p)))
        def _():
            to_side(i).wait_recv()
            total[t, rows] += side_in[i].astype(jnp.float32)

        @pl.when(jnp.logical_not(r["root"]))
        def _():
            tree_out[i] = total[t, rows].astype(jnp.bfloat16)

        @pl.when(falls(p))
        def _():
            to_down(i).start()

        @pl.when(crosses(p))
        def _():
            to_side(i).start()

    for i in range(CHUNKS):
        to_sibling(i).start()
    hops = offsets(n)
    for step, k in enumerate(hops):
        if step >= WINDOW:
            send(hops[step - WINDOW]).wait_send()
        send(k).start()
        halo_starts(r, step, to_halo)
        for p in range(2):
            top = n // STRIDE - 1
            lag = jnp.where(trunk(p), 3 + 2 * (top - r["rung"]), 1)
            if p == 1:
                lag = jnp.where(r["root"], 5 + 2 * top, lag)
            i = step - lag

            @pl.when(jnp.logical_and(jnp.logical_and(i >= 0, i < CHUNKS), lax.rem(i + 2 * n, 2) == p))
            def _(i=i, p=p):
                add(i, p)

    self_copy = pltpu.make_async_copy(outbox.at[me], returned.at[me], table)
    self_copy.start()
    for k in hops[-WINDOW:]:
        send(k).wait_send()
    for k in hops:
        sent(k).wait_recv()
    for i in range(CHUNKS):
        to_sibling(i).wait_send()

        @pl.when(falls(i % 2))
        def _(i=i):
            to_down(i).wait_send()

        @pl.when(crosses(i % 2))
        def _(i=i):
            to_side(i).wait_send()

    self_copy.wait()
    halo_waits(r, to_halo)


def collect(outbox, window, sinks, n, most):
    dma = pltpu.SemaphoreType.DMA
    part = pltpu.VMEM((CHUNKS, ROWS, WIDTH), jnp.bfloat16)
    return pl.pallas_call(
        functools.partial(collect_kernel, n),
        out_shape=(
            jax.ShapeDtypeStruct((n, most, 2, BLK, HD), jnp.bfloat16),
            jax.ShapeDtypeStruct((2, 2, BLK, WIDTH), jnp.bfloat16),
            jax.ShapeDtypeStruct((2, BLK, WIDTH), jnp.float32),
        ),
        in_specs=[ANY, ANY, VMEM],
        out_specs=(ANY, ANY, VMEM),
        scratch_shapes=[part] * 4 + [dma, dma((n,)), dma((n,))] + [dma((CHUNKS,))] * 5 + [dma((2, 2))] * 2,
        compiler_params=pltpu.CompilerParams(
            collective_id=1, has_side_effects=True, vmem_limit_bytes=48 << 20),
        name="collect",
    )(outbox, window, sinks)


def dot(a, b, da, db):
    return lax.dot_general(a, b, (((da,), (db,)), ((), ())), preferred_element_type=jnp.float32)


def core_kernel(n, where, q_ref, g_ref, k_ref, v_ref, near, far0, far1, far2,
                gq_ref, own_ref, window_ref, sink_ref, outbox, terms, sem):
    h = pl.program_id(0)
    slot = lax.rem(h, 2)
    me = where[6 * H]
    lower, upper = me > 0, me < n - 1
    q, g = q_ref[...], g_ref[...]
    zero = jnp.zeros((BLK, HD), jnp.bfloat16)

    def sends(s, hh):
        return [
            pltpu.make_async_copy(
                terms.at[s, j], outbox.at[where[3 * hh + j], where[3 * H + 3 * hh + j]], sem.at[s, j])
            for j in range(3)
        ]

    ks, vs = [], []
    for t, out in ((0, ks), (1, vs)):
        out.append(jnp.where(lower, near[0, t], zero))
        out.append((k_ref, v_ref)[t][...])
        out.append(jnp.where(upper, near[1, t], zero))
        out.append(near[2, t])
        out.append(near[3, t])
        out += [f[0, 0, t] for f in (far0, far1, far2)]
    kc = jnp.concatenate(ks, axis=0)
    vc = jnp.concatenate(vs, axis=0)
    s = dot(kc, q, 1, 1) * SCALE
    row = lax.broadcasted_iota(jnp.int32, (8 * BLK, BLK), 0)
    first = jnp.where(lower, 0, BLK)
    skip = jnp.where(upper, 8 * BLK, 2 * BLK)
    ok = (row >= first) & ((row < skip) | (row >= 3 * BLK))
    s = jnp.where(ok, s, -jnp.inf)
    m = jnp.max(s, axis=0, keepdims=True)
    e = jnp.exp(s - m)
    p = e * (1.0 / jnp.sum(e, axis=0, keepdims=True))
    pb = p.astype(jnp.bfloat16)
    dp = dot(vc, g, 1, 1)
    delta = jnp.sum(pb.astype(jnp.float32) * dp, axis=0, keepdims=True)
    ds = (p * (dp - delta)).astype(jnp.bfloat16)
    gq_ref[...] = (dot(ds, kc, 0, 0) * SCALE).astype(jnp.bfloat16)
    kt = dot(ds, q, 1, 0) * SCALE
    vt = dot(pb, g, 1, 0)

    @pl.when(h >= 2)
    def _():
        for c in sends(slot, h - 2):
            c.wait()

    for t, term in ((0, kt), (1, vt)):
        def at(j, term=term):
            return term[j * BLK:(j + 1) * BLK]

        window_ref[0, t] = at(0).astype(jnp.bfloat16)
        own_ref[0, t] = at(1)
        window_ref[1, t] = at(2).astype(jnp.bfloat16)
        sink_ref[0, t] = at(3).astype(jnp.bfloat16)
        sink_ref[1, t] = at(4).astype(jnp.bfloat16)
        for j in range(3):
            terms[slot, j, t] = at(5 + j).astype(jnp.bfloat16)
    for c in sends(slot, h):
        c.start()

    @pl.when(h == H - 1)
    def _():
        for c in sends(1 - slot, h - 1) + sends(slot, h):
            c.wait()


def attend(where, q, g, k, v, near, fetched, n, most):
    col = pl.BlockSpec((BLK, HD), lambda h, w: (0, h))

    def far(j):
        return pl.BlockSpec(
            (1, 1, 2, BLK, HD), lambda h, w: (w[3 * h + j], w[3 * H + 3 * h + j], 0, 0, 0))

    return pl.pallas_call(
        functools.partial(core_kernel, n),
        out_shape=(
            jax.ShapeDtypeStruct((BLK, WIDTH), jnp.bfloat16),
            jax.ShapeDtypeStruct((H, 2, BLK, HD), jnp.float32),
            jax.ShapeDtypeStruct((2, 2, BLK, WIDTH), jnp.bfloat16),
            jax.ShapeDtypeStruct((2, 2, BLK, WIDTH), jnp.bfloat16),
            jax.ShapeDtypeStruct((n, most, 2, BLK, HD), jnp.bfloat16),
        ),
        grid_spec=pltpu.PrefetchScalarGridSpec(
            num_scalar_prefetch=1,
            grid=(H,),
            in_specs=[col, col, col, col,
                      pl.BlockSpec((4, 2, BLK, HD), lambda h, w: (0, 0, 0, h)),
                      far(0), far(1), far(2)],
            out_specs=(
                col,
                pl.BlockSpec((1, 2, BLK, HD), lambda h, w: (h, 0, 0, 0)),
                pl.BlockSpec((2, 2, BLK, HD), lambda h, w: (0, 0, 0, h)),
                pl.BlockSpec((2, 2, BLK, HD), lambda h, w: (0, 0, 0, h)),
                ANY,
            ),
            scratch_shapes=[
                pltpu.VMEM((2, 3, 2, BLK, HD), jnp.bfloat16),
                pltpu.SemaphoreType.DMA((2, 3)),
            ],
        ),
        compiler_params=pltpu.CompilerParams(vmem_limit_bytes=48 << 20),
        cost_estimate=pl.CostEstimate(flops=3_000_000_000, bytes_accessed=24 << 20, transcendentals=2 << 20),
        name="attend",
    )(where, q, g, k, v, near, fetched, fetched, fetched)


def combine_kernel(n, most, wanted, own, halo, sinks, returned, gk_ref, gv_ref, acc):
    me = wanted[n * most]
    lower, upper, root = me > 0, me < n - 1, me < 2
    for h in range(H):
        cols = slice(h * HD, (h + 1) * HD)
        for t in range(2):
            acc[h, t] = (
                own[h, t]
                + jnp.where(lower, halo[0, t, :, cols].astype(jnp.float32), 0.0)
                + jnp.where(upper, halo[1, t, :, cols].astype(jnp.float32), 0.0)
                + jnp.where(root, sinks[t, :, cols], 0.0)
            )

    def body(i, _):
        h = wanted[i]

        @pl.when(h >= 0)
        def _():
            acc[h] += returned[i].astype(jnp.float32)

        return 0

    lax.fori_loop(0, n * most, body, 0)
    for h in range(H):
        cols = slice(h * HD, (h + 1) * HD)
        gk_ref[:, cols] = acc[h, 0].astype(jnp.bfloat16)
        gv_ref[:, cols] = acc[h, 1].astype(jnp.bfloat16)


def combine(wanted, own, halo, sinks, returned, n, most):
    out = jax.ShapeDtypeStruct((BLK, WIDTH), jnp.bfloat16)
    return pl.pallas_call(
        functools.partial(combine_kernel, n, most),
        out_shape=(out, out),
        in_specs=[SMEM, VMEM, VMEM, VMEM, VMEM],
        out_specs=(VMEM, VMEM),
        scratch_shapes=[pltpu.VMEM((H, 2, BLK, HD), jnp.float32)],
        compiler_params=pltpu.CompilerParams(vmem_limit_bytes=48 << 20),
        cost_estimate=pl.CostEstimate(flops=4_000_000, bytes_accessed=9 << 20, transcendentals=0),
        name="combine",
    )(wanted, own, halo, sinks, returned.reshape(n * most, 2, BLK, HD))


def per_device(queries, keys, values, grad_out, partners):
    n = lax.axis_size("seq")
    me = lax.axis_index("seq").astype(jnp.int32)
    most = max(2, (3 * H + n - 1) // n)
    items = 3 * H
    dests = partners.reshape(items)
    heads = jnp.arange(items, dtype=jnp.int32) // 3
    order = jnp.arange(items)
    same = (dests[:, None] == dests[None, :]) & (order[None, :] < order[:, None])
    rank = jnp.sum(same.astype(jnp.int32), axis=1)
    places = jnp.arange(n * 128, dtype=jnp.int32)
    hit = places[:, None] == (dests * 128 + rank)[None, :]
    asks = jnp.max(jnp.where(hit, heads[None, :], -1), axis=1).reshape(n, 1, 128)
    near, fetched, wanted = fetch(asks, keys, values, n, most)
    where = jnp.concatenate([dests, rank, me[None]])
    grad_queries, own, window, sinks, outbox = attend(
        where, queries, grad_out, keys, values, near, fetched, n, most)
    returned, halo, total = collect(outbox, window, sinks, n, most)
    table = jnp.concatenate([wanted[:, 0, :most].reshape(-1), me[None]])
    grad_keys, grad_values = combine(table, own, halo, total, returned, n, most)
    return grad_queries, grad_keys, grad_values


def solution(mesh):
    block = P(("groups", "seq"), None)
    return jax.shard_map(
        per_device,
        mesh=mesh,
        in_specs=(block, block, block, block, P(("groups", "seq"), None, None)),
        out_specs=(block, block, block),
        check_vma=False,
    )
```

```python
import functools
import math

import jax
import jax.numpy as jnp
from jax import lax
from jax.experimental import pallas as pl
from jax.experimental.pallas import tpu as pltpu
from jax.sharding import PartitionSpec as P

H = 16
HD = 128
BLK = 128
WIDTH = H * HD
SCALE = 1.0 / math.sqrt(HD)
STRIDE = 4
CHUNKS = 4
WINDOW = 6
ROWS = 2 * BLK // CHUNKS
ANY = pl.BlockSpec(memory_space=pl.ANY)
VMEM = pl.BlockSpec(memory_space=pltpu.VMEM)
SMEM = pl.BlockSpec(memory_space=pltpu.SMEM)


def remote(src, dst, send, recv, target):
    return pltpu.make_async_remote_copy(
        src_ref=src, dst_ref=dst, send_sem=send, recv_sem=recv,
        device_id={"seq": target}, device_id_type=pl.DeviceIdType.MESH,
    )


def signs(n):
    me = lax.axis_index("seq")
    rung = me // STRIDE
    root = me < 2
    column = lax.rem(me, STRIDE) // 2
    return dict(
        me=me,
        core=lax.rem(me, 2),
        sibling=me + 1 - 2 * lax.rem(me, 2),
        lower=me > 0,
        upper=me < n - 1,
        odd=lax.rem(me, 2) == 1,
        even=lax.rem(me, 2) == 0,
        root=root,
        high=me >= STRIDE,
        up=me + STRIDE < n,
        rung=rung,
        column=column,
        across=me + 2 - 4 * column,
    )


def greet(n):
    me = lax.axis_index("seq")
    barrier = pltpu.get_barrier_semaphore()

    def hail(k, _):
        pl.semaphore_signal(barrier, inc=1, device_id={"seq": lax.rem(me + k, n)},
                            device_id_type=pl.DeviceIdType.MESH)
        return 0

    lax.fori_loop(1, n, hail, 0)
    pl.semaphore_wait(barrier, n - 1)


def offsets(n):
    wide = sorted(range(1, n), key=lambda k: (abs(k - n // 2), k))
    out = []
    while wide:
        out.append(wide.pop(0))
        if wide:
            out.append(wide.pop())
    return out


def piece(ref, lead, i):
    half = CHUNKS // 2
    return ref.at[lead, i // half, pl.ds(pl.multiple_of(lax.rem(i, half) * ROWS, ROWS), ROWS)]


def halo_starts(r, step, to_halo):
    early = ((r["even"], True), (r["odd"], False))
    late = ((jnp.logical_and(r["odd"], r["upper"]), True), (jnp.logical_and(r["even"], r["lower"]), False))
    for t in range(2):
        for sides, at in ((early, 0), (late, (3, 8)[t])):
            if step != at:
                continue
            for ok, up in sides:
                @pl.when(ok)
                def _(t=t, up=up):
                    to_halo(t, up).start()


def halo_waits(r, to_halo):
    for t in range(2):
        for ok, up in ((r["upper"], True), (r["lower"], False)):
            @pl.when(ok)
            def _(t=t, up=up):
                to_halo(t, up).wait_send()
        for ok, up in ((r["lower"], True), (r["upper"], False)):
            @pl.when(ok)
            def _(t=t, up=up):
                to_halo(t, up).wait_recv()


def fetch_kernel(n, most, asks, keys, values, near, fetched, wanted, held, ready, picks,
                 load, ask_s, ask_r, table, all_s, all_r, tree_s, tree_r, side_s, sib_s, sib_r,
                 halo_s, halo_r):
    r = signs(n)
    me, core, root = r["me"], r["core"], r["root"]
    loads = []
    for h in range(H):
        cols = pl.ds(h * HD, HD)
        loads.append(pltpu.make_async_copy(keys.at[:, cols], held.at[h, 0], load.at[h, 0]))
        loads.append(pltpu.make_async_copy(values.at[:, cols], held.at[h, 1], load.at[h, 1]))
    for c in loads:
        c.start()
    greet(n)

    def ask(k):
        peer = lax.rem(me + k, n)
        return remote(asks.at[peer], wanted.at[me], ask_s.at[peer], ask_r.at[me], peer)

    def asked(k):
        peer = lax.rem(me + k, n)
        return remote(asks.at[peer], wanted.at[peer], ask_s.at[peer], ask_r.at[peer], peer)

    for k in range(1, n):
        ask(k).start()
    mine = pltpu.make_async_copy(asks.at[me], wanted.at[me], table)
    mine.start()

    def own(t, i):
        return (keys, values)[t].at[pl.ds(pl.multiple_of(lax.rem(i, CHUNKS // 2) * ROWS, ROWS), ROWS)]

    def to_up(i, src):
        return remote(src, piece(near, 2 + core, i), tree_s.at[i], tree_r.at[i], me + STRIDE)

    def to_side(i, src):
        return remote(src, piece(near, 2 + core, i), side_s.at[i], tree_r.at[i], r["across"])

    def to_sibling(i, src):
        return remote(src, piece(near, 2 + core, i), sib_s.at[i], sib_r.at[i], r["sibling"])

    def from_sibling(i):
        return remote(piece(near, 3 - core, i), piece(near, 3 - core, i), sib_s.at[i], sib_r.at[i], r["sibling"])

    def keep(t):
        return pltpu.make_async_copy((keys, values)[t], near.at[2 + core, t], load.at[t, 0])

    def to_halo(t, up):
        slot = 0 if up else 1
        return remote((keys, values)[t], near.at[slot, t], halo_s.at[slot, t], halo_r.at[slot, t],
                      me + (1 if up else -1))

    def rises(p):
        return jnp.logical_and(r["up"], r["column"] == p)

    def crosses(p):
        return jnp.logical_or(root, jnp.logical_and(r["high"], r["column"] == p))

    def relay(i, p):
        for t in range(2):
            @pl.when(jnp.logical_and(root, i // (CHUNKS // 2) == t))
            def _(t=t):
                @pl.when(rises(p))
                def _():
                    to_up(i, own(t, i)).start()

                to_side(i, own(t, i)).start()
                to_sibling(i, own(t, i)).start()

        @pl.when(jnp.logical_not(root))
        def _():
            to_up(i, piece(near, 2 + core, i)).wait_recv()

            @pl.when(rises(p))
            def _():
                to_up(i, piece(near, 2 + core, i)).start()

            @pl.when(crosses(p))
            def _():
                to_side(i, piece(near, 2 + core, i)).start()

            to_sibling(i, piece(near, 2 + core, i)).start()

    def relay_at(step):
        for p in range(2):
            lag = 2 * r["rung"] + (2 * r["column"] if p == 0 else 3 - r["column"])
            i = step - jnp.where(root, 0, lag)

            @pl.when(jnp.logical_and(jnp.logical_and(i >= 0, i < CHUNKS), lax.rem(i + 2 * n, 2) == p))
            def _(i=i, p=p):
                relay(i, p)

    relay_at(0)
    halo_starts(r, 0, to_halo)
    for c in loads:
        c.wait()

    @pl.when(root)
    def _():
        for t in range(2):
            keep(t).start()

    for k in range(1, n):
        asked(k).wait_recv()
    mine.wait()
    copy = pltpu.make_async_copy(wanted, picks, table)
    copy.start()
    copy.wait()

    def fill(peer):
        for j in range(most):
            ready[peer, j] = held[jnp.maximum(picks[peer, 0, j], 0)]

    def send(k):
        peer = lax.rem(me + k, n)
        return remote(ready.at[peer], fetched.at[me], all_s.at[peer], all_r.at[me], peer)

    def sent(k):
        peer = lax.rem(me + k, n)
        return remote(ready.at[peer], fetched.at[peer], all_s.at[peer], all_r.at[peer], peer)

    hops = offsets(n)
    for step, k in enumerate(hops):
        fill(lax.rem(me + k, n))
        if step >= WINDOW:
            send(hops[step - WINDOW]).wait_send()
        send(k).start()
        if step:
            relay_at(step)
            halo_starts(r, step, to_halo)
    fill(me)
    self_copy = pltpu.make_async_copy(ready.at[me], fetched.at[me], table)
    self_copy.start()
    for k in hops[-WINDOW:]:
        send(k).wait_send()
    for k in hops:
        sent(k).wait_recv()
    for k in range(1, n):
        ask(k).wait_send()
    for i in range(CHUNKS):
        from_sibling(i).wait_recv()
        to_sibling(i, piece(near, 2 + core, i)).wait_send()

        @pl.when(rises(i % 2))
        def _(i=i):
            to_up(i, piece(near, 2 + core, i)).wait_send()

        @pl.when(crosses(i % 2))
        def _(i=i):
            to_side(i, piece(near, 2 + core, i)).wait_send()

    @pl.when(root)
    def _():
        for t in range(2):
            keep(t).wait()

    self_copy.wait()
    halo_waits(r, to_halo)


def fetch(asks, keys, values, n, most):
    dma = pltpu.SemaphoreType.DMA
    return pl.pallas_call(
        functools.partial(fetch_kernel, n, most),
        out_shape=(
            jax.ShapeDtypeStruct((4, 2, BLK, WIDTH), jnp.bfloat16),
            jax.ShapeDtypeStruct((n, most, 2, BLK, HD), jnp.bfloat16),
            jax.ShapeDtypeStruct((n, 1, 128), jnp.int32),
        ),
        in_specs=[VMEM, ANY, ANY],
        out_specs=(ANY, ANY, VMEM),
        scratch_shapes=[
            pltpu.VMEM((H, 2, BLK, HD), jnp.bfloat16),
            pltpu.VMEM((n, most, 2, BLK, HD), jnp.bfloat16),
            pltpu.SMEM((n, 1, 128), jnp.int32),
            dma((H, 2)), dma((n,)), dma((n,)), dma, dma((n,)), dma((n,)),
            dma((CHUNKS,)), dma((CHUNKS,)), dma((CHUNKS,)), dma((CHUNKS,)), dma((CHUNKS,)),
            dma((2, 2)), dma((2, 2)),
        ],
        compiler_params=pltpu.CompilerParams(
            collective_id=0, has_side_effects=True, vmem_limit_bytes=60 << 20),
        name="fetch",
    )(asks, keys, values)


def collect_kernel(n, outbox, window, sinks, returned, halo, total, sib_in, tree_in, side_in, tree_out,
                   table, all_s, all_r, tree_s, tree_r, side_r, sib_s, sib_r, halo_s, halo_r):
    r = signs(n)
    me, core = r["me"], r["core"]
    greet(n)

    def to_sibling(i):
        return remote(piece(sinks, 1 - core, i), sib_in.at[i], sib_s.at[i], sib_r.at[i], r["sibling"])

    def to_down(i):
        return remote(tree_out.at[i], tree_in.at[i], tree_s.at[i], tree_r.at[i], me - STRIDE)

    def to_side(i):
        return remote(tree_out.at[i], side_in.at[i], tree_s.at[i], side_r.at[i], r["across"])

    def to_halo(t, up):
        slot = 0 if up else 1
        return remote(window.at[1 - slot, t], halo.at[slot, t],
                      halo_s.at[slot, t], halo_r.at[slot, t], me + (1 if up else -1))

    def send(k):
        peer = lax.rem(me + k, n)
        return remote(outbox.at[peer], returned.at[me], all_s.at[peer], all_r.at[me], peer)

    def sent(k):
        peer = lax.rem(me + k, n)
        return remote(outbox.at[peer], returned.at[peer], all_s.at[peer], all_r.at[peer], peer)

    def trunk(p):
        return r["column"] == p

    def falls(p):
        return jnp.logical_and(trunk(p), r["high"])

    def crosses(p):
        return jnp.logical_not(jnp.logical_or(r["root"], falls(p)))

    def add(i, p):
        half = CHUNKS // 2
        t, rows = i // half, pl.ds(pl.multiple_of(lax.rem(i, half) * ROWS, ROWS), ROWS)
        to_sibling(i).wait_recv()
        total[t, rows] = sinks[core, t, rows].astype(jnp.float32) + sib_in[i].astype(jnp.float32)

        @pl.when(jnp.logical_and(r["up"], trunk(p)))
        def _():
            to_down(i).wait_recv()
            total[t, rows] += tree_in[i].astype(jnp.float32)

        @pl.when(jnp.logical_or(r["root"], falls(p)))
        def _():
            to_side(i).wait_recv()
            total[t, rows] += side_in[i].astype(jnp.float32)

        @pl.when(jnp.logical_not(r["root"]))
        def _():
            tree_out[i] = total[t, rows].astype(jnp.bfloat16)

        @pl.when(falls(p))
        def _():
            to_down(i).start()

        @pl.when(crosses(p))
        def _():
            to_side(i).start()

    for i in range(CHUNKS):
        to_sibling(i).start()
    hops = offsets(n)
    for step, k in enumerate(hops):
        if step >= WINDOW:
            send(hops[step - WINDOW]).wait_send()
        send(k).start()
        halo_starts(r, step, to_halo)
        for p in range(2):
            top = n // STRIDE - 1
            lag = jnp.where(trunk(p), 3 + 2 * (top - r["rung"]), 1)
            if p == 1:
                lag = jnp.where(r["root"], 5 + 2 * top, lag)
            i = step - lag

            @pl.when(jnp.logical_and(jnp.logical_and(i >= 0, i < CHUNKS), lax.rem(i + 2 * n, 2) == p))
            def _(i=i, p=p):
                add(i, p)

    self_copy = pltpu.make_async_copy(outbox.at[me], returned.at[me], table)
    self_copy.start()
    for k in hops[-WINDOW:]:
        send(k).wait_send()
    for k in hops:
        sent(k).wait_recv()
    for i in range(CHUNKS):
        to_sibling(i).wait_send()

        @pl.when(falls(i % 2))
        def _(i=i):
            to_down(i).wait_send()

        @pl.when(crosses(i % 2))
        def _(i=i):
            to_side(i).wait_send()

    self_copy.wait()
    halo_waits(r, to_halo)


def collect(outbox, window, sinks, n, most):
    dma = pltpu.SemaphoreType.DMA
    part = pltpu.VMEM((CHUNKS, ROWS, WIDTH), jnp.bfloat16)
    return pl.pallas_call(
        functools.partial(collect_kernel, n),
        out_shape=(
            jax.ShapeDtypeStruct((n, most, 2, BLK, HD), jnp.bfloat16),
            jax.ShapeDtypeStruct((2, 2, BLK, WIDTH), jnp.bfloat16),
            jax.ShapeDtypeStruct((2, BLK, WIDTH), jnp.float32),
        ),
        in_specs=[ANY, ANY, VMEM],
        out_specs=(ANY, ANY, VMEM),
        scratch_shapes=[part] * 4 + [dma, dma((n,)), dma((n,))] + [dma((CHUNKS,))] * 5 + [dma((2, 2))] * 2,
        compiler_params=pltpu.CompilerParams(
            collective_id=1, has_side_effects=True, vmem_limit_bytes=60 << 20),
        name="collect",
    )(outbox, window, sinks)


def dot(a, b, da, db):
    return lax.dot_general(a, b, (((da,), (db,)), ((), ())), preferred_element_type=jnp.float32)


def core_kernel(n, where, q_ref, g_ref, k_ref, v_ref, near, far0, far1, far2,
                gq_ref, own_ref, window_ref, sink_ref, outbox, terms, sem):
    h = pl.program_id(0)
    slot = lax.rem(h, 2)
    me = where[6 * H]
    lower, upper = me > 0, me < n - 1
    q, g = q_ref[...], g_ref[...]
    zero = jnp.zeros((BLK, HD), jnp.bfloat16)

    def sends(s, hh):
        return [
            pltpu.make_async_copy(
                terms.at[s, j], outbox.at[where[3 * hh + j], where[3 * H + 3 * hh + j]], sem.at[s, j])
            for j in range(3)
        ]

    ks, vs = [], []
    for t, out in ((0, ks), (1, vs)):
        out.append(jnp.where(lower, near[0, t], zero))
        out.append((k_ref, v_ref)[t][...])
        out.append(jnp.where(upper, near[1, t], zero))
        out.append(near[2, t])
        out.append(near[3, t])
        out += [f[0, 0, t] for f in (far0, far1, far2)]
    kc = jnp.concatenate(ks, axis=0)
    vc = jnp.concatenate(vs, axis=0)
    s = dot(kc, q, 1, 1) * SCALE
    row = lax.broadcasted_iota(jnp.int32, (8 * BLK, BLK), 0)
    first = jnp.where(lower, 0, BLK)
    skip = jnp.where(upper, 8 * BLK, 2 * BLK)
    ok = (row >= first) & ((row < skip) | (row >= 3 * BLK))
    s = jnp.where(ok, s, -jnp.inf)
    m = jnp.max(s, axis=0, keepdims=True)
    e = jnp.exp(s - m)
    p = e * (1.0 / jnp.sum(e, axis=0, keepdims=True))
    pb = p.astype(jnp.bfloat16)
    dp = dot(vc, g, 1, 1)
    delta = jnp.sum(pb.astype(jnp.float32) * dp, axis=0, keepdims=True)
    ds = (p * (dp - delta)).astype(jnp.bfloat16)
    gq_ref[...] = (dot(ds, kc, 0, 0) * SCALE).astype(jnp.bfloat16)
    kt = dot(ds, q, 1, 0) * SCALE
    vt = dot(pb, g, 1, 0)

    @pl.when(h >= 2)
    def _():
        for c in sends(slot, h - 2):
            c.wait()

    for t, term in ((0, kt), (1, vt)):
        def at(j, term=term):
            return term[j * BLK:(j + 1) * BLK]

        window_ref[0, t] = at(0).astype(jnp.bfloat16)
        own_ref[0, t] = at(1)
        window_ref[1, t] = at(2).astype(jnp.bfloat16)
        sink_ref[0, t] = at(3).astype(jnp.bfloat16)
        sink_ref[1, t] = at(4).astype(jnp.bfloat16)
        for j in range(3):
            terms[slot, j, t] = at(5 + j).astype(jnp.bfloat16)
    for c in sends(slot, h):
        c.start()

    @pl.when(h == H - 1)
    def _():
        for c in sends(1 - slot, h - 1) + sends(slot, h):
            c.wait()


def attend(where, q, g, k, v, near, fetched, n, most):
    col = pl.BlockSpec((BLK, HD), lambda h, w: (0, h))

    def far(j):
        return pl.BlockSpec(
            (1, 1, 2, BLK, HD), lambda h, w: (w[3 * h + j], w[3 * H + 3 * h + j], 0, 0, 0))

    return pl.pallas_call(
        functools.partial(core_kernel, n),
        out_shape=(
            jax.ShapeDtypeStruct((BLK, WIDTH), jnp.bfloat16),
            jax.ShapeDtypeStruct((H, 2, BLK, HD), jnp.float32),
            jax.ShapeDtypeStruct((2, 2, BLK, WIDTH), jnp.bfloat16),
            jax.ShapeDtypeStruct((2, 2, BLK, WIDTH), jnp.bfloat16),
            jax.ShapeDtypeStruct((n, most, 2, BLK, HD), jnp.bfloat16),
        ),
        grid_spec=pltpu.PrefetchScalarGridSpec(
            num_scalar_prefetch=1,
            grid=(H,),
            in_specs=[col, col, col, col,
                      pl.BlockSpec((4, 2, BLK, HD), lambda h, w: (0, 0, 0, h)),
                      far(0), far(1), far(2)],
            out_specs=(
                col,
                pl.BlockSpec((1, 2, BLK, HD), lambda h, w: (h, 0, 0, 0)),
                pl.BlockSpec((2, 2, BLK, HD), lambda h, w: (0, 0, 0, h)),
                pl.BlockSpec((2, 2, BLK, HD), lambda h, w: (0, 0, 0, h)),
                ANY,
            ),
            scratch_shapes=[
                pltpu.VMEM((2, 3, 2, BLK, HD), jnp.bfloat16),
                pltpu.SemaphoreType.DMA((2, 3)),
            ],
        ),
        compiler_params=pltpu.CompilerParams(vmem_limit_bytes=60 << 20),
        cost_estimate=pl.CostEstimate(flops=3_000_000_000, bytes_accessed=24 << 20, transcendentals=2 << 20),
        name="attend",
    )(where, q, g, k, v, near, fetched, fetched, fetched)


def combine_kernel(n, most, wanted, own, halo, sinks, returned, gk_ref, gv_ref, acc):
    me = wanted[n * most]
    lower, upper, root = me > 0, me < n - 1, me < 2
    for h in range(H):
        cols = slice(h * HD, (h + 1) * HD)
        for t in range(2):
            acc[h, t] = (
                own[h, t]
                + jnp.where(lower, halo[0, t, :, cols].astype(jnp.float32), 0.0)
                + jnp.where(upper, halo[1, t, :, cols].astype(jnp.float32), 0.0)
                + jnp.where(root, sinks[t, :, cols], 0.0)
            )

    def body(i, _):
        h = wanted[i]

        @pl.when(h >= 0)
        def _():
            acc[h] += returned[i].astype(jnp.float32)

        return 0

    lax.fori_loop(0, n * most, body, 0)
    for h in range(H):
        cols = slice(h * HD, (h + 1) * HD)
        gk_ref[:, cols] = acc[h, 0].astype(jnp.bfloat16)
        gv_ref[:, cols] = acc[h, 1].astype(jnp.bfloat16)


def combine(wanted, own, halo, sinks, returned, n, most):
    out = jax.ShapeDtypeStruct((BLK, WIDTH), jnp.bfloat16)
    return pl.pallas_call(
        functools.partial(combine_kernel, n, most),
        out_shape=(out, out),
        in_specs=[SMEM, VMEM, VMEM, VMEM, VMEM],
        out_specs=(VMEM, VMEM),
        scratch_shapes=[pltpu.VMEM((H, 2, BLK, HD), jnp.float32)],
        compiler_params=pltpu.CompilerParams(vmem_limit_bytes=60 << 20),
        cost_estimate=pl.CostEstimate(flops=4_000_000, bytes_accessed=9 << 20, transcendentals=0),
        name="combine",
    )(wanted, own, halo, sinks, returned.reshape(n * most, 2, BLK, HD))


def per_device(queries, keys, values, grad_out, partners):
    n = lax.axis_size("seq")
    me = lax.axis_index("seq").astype(jnp.int32)
    most = max(2, (3 * H + n - 1) // n)
    items = 3 * H
    dests = partners.reshape(items)
    heads = jnp.arange(items, dtype=jnp.int32) // 3
    order = jnp.arange(items)
    same = (dests[:, None] == dests[None, :]) & (order[None, :] < order[:, None])
    rank = jnp.sum(same.astype(jnp.int32), axis=1)
    places = jnp.arange(n * 128, dtype=jnp.int32)
    hit = places[:, None] == (dests * 128 + rank)[None, :]
    asks = jnp.max(jnp.where(hit, heads[None, :], -1), axis=1).reshape(n, 1, 128)
    near, fetched, wanted = fetch(asks, keys, values, n, most)
    where = jnp.concatenate([dests, rank, me[None]])
    grad_queries, own, window, sinks, outbox = attend(
        where, queries, grad_out, keys, values, near, fetched, n, most)
    returned, halo, total = collect(outbox, window, sinks, n, most)
    table = jnp.concatenate([wanted[:, 0, :most].reshape(-1), me[None]])
    grad_keys, grad_values = combine(table, own, halo, total, returned, n, most)
    return grad_queries, grad_keys, grad_values


def solution(mesh):
    block = P(("groups", "seq"), None)
    return jax.shard_map(
        per_device,
        mesh=mesh,
        in_specs=(block, block, block, block, P(("groups", "seq"), None, None)),
        out_specs=(block, block, block),
        check_vma=False,
    )
```
